32 devices in a mesh: section: 2 (over core), ctx: 4 (over y, x), wt: 4 (over z).
Axes of the slice: x: 2, y: 2, z: 4, core: 2. Of those that a mesh axis runs over, the one named last changes fastest.
Arguments:
- hidden_in: bfloat16 [4, 512, 2560], P(None, 'ctx', 'wt'), may hold values from -6 to 6
- out_grad: bfloat16 [4, 512, 2560], P(None, 'ctx', 'wt'), may hold values from -6 to 6
- block_pos: int32 [4, 8], replicated, may hold values from 0 to 7, as said below
- norm1_gain: float32 [2, 2560], P('section', 'wt'), may hold values from 0.25 to 1.75
- norm2_gain: float32 [2, 2560], P('section', 'wt'), may hold values from 0.25 to 1.75
- wq: bfloat16 [2, 2560, 2560], P('section', 'wt'), as said below
- wk: bfloat16 [2, 2560, 256], P('section', 'wt'), as said below
- wv: bfloat16 [2, 2560, 256], P('section', 'wt'), may hold values from -0.125 to 0.125
- wo: bfloat16 [2, 2560, 2560], P('section', None, 'wt'), may hold values from -2 to 2
- w_gate: bfloat16 [2, 2560, 7680], P('section', None, 'wt'), may hold values from -0.125 to 0.125
- w_up: bfloat16 [2, 2560, 7680], P('section', None, 'wt'), may hold values from -0.125 to 0.125
- w_down: bfloat16 [2, 7680, 2560], P('section', 'wt'), may hold values from -0.0625 to 0.0625
Outputs:
- out: bfloat16 [4, 512, 2560], P(None, 'ctx', 'wt')
- in_grad: float32 [4, 512, 2560], P(None, 'ctx', 'wt')
- grad_wq: float32 [2, 2560, 2560], P('section', 'wt', 'ctx')
- grad_wk: float32 [2, 2560, 256], P('section', 'wt', 'ctx')
- grad_wv: float32 [2, 2560, 256], P('section', 'wt', 'ctx')
- grad_wo: float32 [2, 2560, 2560], P('section', 'ctx', 'wt')
- grad_gate: float32 [2, 2560, 7680], P('section', 'ctx', 'wt')
- grad_up: float32 [2, 2560, 7680], P('section', 'ctx', 'wt')
- grad_down: float32 [2, 7680, 2560], P('section', 'wt', 'ctx')
- grad_gain1: float32 [2, 2560], P('section', 'wt')
- grad_gain2: float32 [2, 2560], P('section', 'wt')
The draws below stay inside these ranges and needn't reach their ends.
Inputs may be any that keep to these rules, and one draw needn't show every extreme that they name: `block_pos`: in every micro-batch's row each block number appears once, and the entries at places 2 * c and 2 * c + 1 add up to 7. `wq`: entries are of order 2560 ** -0.5 times a factor of at most 16. `wk`: entries are of order 2560 ** -0.5.
All inputs are finite; a program needn't handle non-finite values.
Results may differ from the reference program's by a relative error of at most 0.028.
Values may be sent and summed in bfloat16 or wider, within the bound.
No kernel may reach another device: no remote copies, remote signals or barrier semaphores. Data moves between devices by JAX's collectives and lax.ppermute only.
A program may use at most 576 MiB of HBM per device.

```python
import math
import jax
import jax.numpy as jnp
from jax import lax

D = 2560
HEADS = 10
HD = 256
FF = 7680
MICRO = 4
HQ = 2560
SEQ = 512
BLK = 64
BLOCKS = 8
N_CTX = 4


def attention_pair(base_key):
    key_draw = jax.random.fold_in(base_key, 101)
    query_draw = jax.random.fold_in(base_key, 202)
    scale_value = D ** (-0.5)
    key_weights = jax.random.truncated_normal(key_draw, -4.0, 4.0, (2, D, HD), jnp.float32) * scale_value
    query_weights = jax.random.truncated_normal(query_draw, -4.0, 4.0, (2, D, HEADS * HD), jnp.float32) * scale_value
    return (query_weights, key_weights)


def draw_wq(key, part):
    return attention_pair(key)[0].astype(jnp.bfloat16)


def draw_wk(key, part):
    return attention_pair(key)[1].astype(jnp.bfloat16)


def draw_block_pos(key, part):
    micro_keys = jax.random.split(jax.random.fold_in(key, 7), MICRO)
    lower = jax.vmap(lambda one_key: jax.random.permutation(one_key, N_CTX))(micro_keys).astype(jnp.int32)
    flips = jax.random.randint(jax.random.fold_in(key, 8), (MICRO, N_CTX), 0, 2)
    upper = BLOCKS - 1 - lower
    leading = jnp.where(flips == 1, upper, lower)
    trailing = jnp.where(flips == 1, lower, upper)
    return jnp.stack([leading, trailing], axis=2).reshape(MICRO, BLOCKS).astype(jnp.int32)


def steps_of(stream_key, shape, pieces, smallest, top_value):
    factor_of = 1.0
    for axis_at, blocks in pieces:
        steps = jax.random.uniform(jax.random.fold_in(jax.random.fold_in(stream_key, 6), axis_at), (blocks,), jnp.float32, smallest / len(pieces), top_value / len(pieces))
        factor_of = factor_of * jnp.repeat(jnp.exp(steps), shape[axis_at] // blocks).reshape((-1,) + (1,) * (len(shape) - 1 - axis_at))
    return factor_of


def scatter_about(own_key, shape, width, bound, pieces=(), held_as=jnp.bfloat16):
    values = width * jax.random.normal(own_key, shape, jnp.float32)
    if pieces:
        values = values * steps_of(own_key, shape, pieces, -0.22, 0.18)
    return jnp.clip(values, -bound, bound).astype(held_as)


def setup_inputs(seed: int = 0) -> dict:
    key_list = jax.random.split(jax.random.key(seed), 13)
    hidden_in = scatter_about(key_list[0], (MICRO, SEQ, D), 1.0, 6.0, ((1, 4), (2, 4)))
    out_grad = scatter_about(key_list[1], (MICRO, SEQ, D), 1.0, 6.0, ((1, 4), (2, 4)))
    block_pos = draw_block_pos(jax.random.fold_in(key_list[12], 71), 0)
    norm1_gain = jnp.clip(1.0 + 0.15 * jax.random.normal(key_list[3], (2, D), jnp.float32), 0.25, 1.75)
    norm2_gain = jnp.clip(1.0 + 0.15 * jax.random.normal(key_list[4], (2, D), jnp.float32), 0.25, 1.75)
    wq = draw_wq(jax.random.fold_in(key_list[12], 71), 0)
    wk = draw_wk(jax.random.fold_in(key_list[12], 71), 0)
    wv = scatter_about(key_list[7], (2, D, HD), D ** -0.5, 0.125, ((0, 2), (1, 4)))
    wo = scatter_about(key_list[8], (2, HQ, D), (max(1, 2 * HQ // SEQ)) ** -0.5, 2.0, ((0, 2), (2, 4)))
    w_gate = scatter_about(key_list[9], (2, D, FF), D ** -0.5, 0.125, ((0, 2), (2, 4)))
    w_up = scatter_about(key_list[10], (2, D, FF), D ** -0.5, 0.125, ((0, 2), (2, 4)))
    w_down = scatter_about(key_list[11], (2, FF, D), FF ** -0.5, 0.0625, ((0, 2), (1, 4)))
    return {"hidden_in": hidden_in, "out_grad": out_grad, "block_pos": block_pos, "norm1_gain": norm1_gain, "norm2_gain": norm2_gain, "wq": wq, "wk": wk, "wv": wv, "wo": wo, "w_gate": w_gate, "w_up": w_up, "w_down": w_down}


EPS = 1e-06
ROPE_LOG = math.log(10000.0)
NEG_FILL = -1e+30

def gelu_tanh(values):
    return jax.nn.gelu(values, approximate=True)

def rotate(values, positions, direction):
    half_size = values.shape[-1] // 2
    freqs = jnp.exp(jnp.arange(half_size, dtype=jnp.float32) * (-2.0 * ROPE_LOG / values.shape[-1]))
    angles = positions.astype(jnp.float32)[:, None, None] * freqs
    cosine = jnp.cos(angles)
    sine = jnp.sin(angles) * direction
    first_half = values[..., :half_size]
    second_half = values[..., half_size:]
    return jnp.concatenate([first_half * cosine - second_half * sine, second_half * cosine + first_half * sine], axis=-1)

def positions_for(block_row, seq_len, block_len):
    places = jnp.arange(seq_len, dtype=jnp.int32)
    owners = (places // block_len)[:, None] == jnp.arange(block_row.shape[0], dtype=jnp.int32)[None, :]
    return lax.optimization_barrier(jnp.sum(jnp.where(owners, block_row[None, :], 0), axis=1)).astype(jnp.int32) * block_len + places % block_len

def masked_scores(query_rows, key_rows, query_pos, key_pos, score_scale):
    raw = jnp.dot(query_rows, key_rows.T, preferred_element_type=jnp.float32) * score_scale
    return jnp.where(key_pos[None, :] <= query_pos[:, None], raw, NEG_FILL)

def norm_backward(d_normed, source, inverse, gain, carried):
    scaled = d_normed * gain
    inner = lax.optimization_barrier(jnp.mean(scaled * source, axis=1))
    d_source = carried + inverse[:, None] * scaled - source * (inverse ** 3 * inner)[:, None]
    d_gain = lax.optimization_barrier(jnp.sum(d_normed * source * inverse[:, None], axis=0))
    return (d_gain, d_source)

def block_forward(source, positions, weights):
    gain_first, gain_second, w_query, w_key, w_value, w_out, w_gate_l, w_up_l, w_down_l = weights
    inv_first = lax.rsqrt(lax.optimization_barrier(jnp.mean(source * source, axis=1)) + EPS)
    normed_first = (source * inv_first[:, None] * gain_first).astype(jnp.bfloat16)
    query_pre = jnp.dot(normed_first, w_query, preferred_element_type=jnp.float32)
    key_pre = jnp.dot(normed_first, w_key, preferred_element_type=jnp.float32)
    value_pre = jnp.dot(normed_first, w_value, preferred_element_type=jnp.float32)
    queries = rotate(query_pre.reshape(SEQ, HEADS, HD), positions, 1.0).astype(jnp.bfloat16)
    key_rows = rotate(key_pre[:, None, :], positions, 1.0)[:, 0].astype(jnp.bfloat16)
    value_rows = value_pre.astype(jnp.bfloat16)
    score_scale = HD ** (-0.5)

    def head_forward(head_queries):
        scores = masked_scores(head_queries, key_rows, positions, positions, score_scale)
        row_max = lax.optimization_barrier(jnp.max(scores, axis=1, keepdims=True))
        log_total = row_max[:, 0] + jnp.log(lax.optimization_barrier(jnp.sum(jnp.exp(scores - row_max), axis=1)))
        probs = jnp.exp(scores - log_total[:, None]).astype(jnp.bfloat16)
        return (jnp.dot(probs, value_rows, preferred_element_type=jnp.float32).astype(jnp.bfloat16), log_total)
    head_out, log_totals = lax.map(head_forward, jnp.transpose(queries, (1, 0, 2)))
    attended = jnp.transpose(head_out, (1, 0, 2)).reshape(SEQ, HEADS * HD)
    middle = source + jnp.dot(attended, w_out, preferred_element_type=jnp.float32)
    inv_second = lax.rsqrt(lax.optimization_barrier(jnp.mean(middle * middle, axis=1)) + EPS)
    normed_second = (middle * inv_second[:, None] * gain_second).astype(jnp.bfloat16)
    gate_pre = jnp.dot(normed_second, w_gate_l, preferred_element_type=jnp.float32)
    up_pre = jnp.dot(normed_second, w_up_l, preferred_element_type=jnp.float32)
    hidden_act = (gelu_tanh(gate_pre) * up_pre).astype(jnp.bfloat16)
    result = middle + jnp.dot(hidden_act, w_down_l, preferred_element_type=jnp.float32)
    saved_state = (source, inv_first, normed_first, queries, key_rows, value_rows, log_totals, attended, middle, inv_second, normed_second, gate_pre, up_pre)
    return (result, saved_state)

def block_backward(grad_out, saved_state, positions, weights):
    gain_first, gain_second, w_query, w_key, w_value, w_out, w_gate_l, w_up_l, w_down_l = weights
    source, inv_first, normed_first, queries, key_rows, value_rows, log_totals, attended, middle, inv_second, normed_second, gate_pre, up_pre = saved_state
    score_scale = HD ** (-0.5)
    grad_low = grad_out.astype(jnp.bfloat16)
    hidden_act = (gelu_tanh(gate_pre) * up_pre).astype(jnp.bfloat16)
    d_down = jnp.dot(hidden_act.T, grad_low, preferred_element_type=jnp.float32)
    d_hidden = jnp.dot(grad_low, w_down_l.T, preferred_element_type=jnp.float32)
    activated, pull_back = jax.vjp(gelu_tanh, gate_pre)
    d_gate_pre = pull_back(d_hidden * up_pre)[0].astype(jnp.bfloat16)
    d_up_pre = (d_hidden * activated).astype(jnp.bfloat16)
    d_gate_w = jnp.dot(normed_second.T, d_gate_pre, preferred_element_type=jnp.float32)
    d_up_w = jnp.dot(normed_second.T, d_up_pre, preferred_element_type=jnp.float32)
    d_normed_second = jnp.dot(d_gate_pre, w_gate_l.T, preferred_element_type=jnp.float32) + jnp.dot(d_up_pre, w_up_l.T, preferred_element_type=jnp.float32)
    d_gain_second, d_middle = norm_backward(d_normed_second, middle, inv_second, gain_second, grad_out)
    d_middle_low = d_middle.astype(jnp.bfloat16)
    d_out_w = jnp.dot(attended.T, d_middle_low, preferred_element_type=jnp.float32)
    d_attended = jnp.dot(d_middle_low, w_out.T, preferred_element_type=jnp.float32).astype(jnp.bfloat16)

    def head_backward(head_args):
        head_queries, head_total, head_grad = head_args
        scores = masked_scores(head_queries, key_rows, positions, positions, score_scale)
        probs = jnp.exp(scores - head_total[:, None])
        probs_low = probs.astype(jnp.bfloat16)
        d_value_head = jnp.dot(probs_low.T, head_grad, preferred_element_type=jnp.float32)
        d_probs = jnp.dot(head_grad, value_rows.T, preferred_element_type=jnp.float32)
        delta_sum = lax.optimization_barrier(jnp.sum(probs * d_probs, axis=1))
        d_scores = (probs * (d_probs - delta_sum[:, None]) * score_scale).astype(jnp.bfloat16)
        d_query_head = jnp.dot(d_scores, key_rows, preferred_element_type=jnp.float32)
        d_key_head = jnp.dot(d_scores.T, head_queries, preferred_element_type=jnp.float32)
        return (d_query_head, d_key_head, d_value_head)
    d_heads = jnp.transpose(d_attended.reshape(SEQ, HEADS, HD), (1, 0, 2))
    d_query_all, d_key_all, d_value_all = lax.map(head_backward, (jnp.transpose(queries, (1, 0, 2)), log_totals, d_heads))
    d_query = rotate(jnp.transpose(d_query_all, (1, 0, 2)), positions, -1.0).reshape(SEQ, HEADS * HD).astype(jnp.bfloat16)
    d_key = rotate(lax.optimization_barrier(jnp.sum(d_key_all, axis=0))[:, None, :], positions, -1.0)[:, 0].astype(jnp.bfloat16)
    d_value = lax.optimization_barrier(jnp.sum(d_value_all, axis=0)).astype(jnp.bfloat16)
    d_query_w = jnp.dot(normed_first.T, d_query, preferred_element_type=jnp.float32)
    d_key_w = jnp.dot(normed_first.T, d_key, preferred_element_type=jnp.float32)
    d_value_w = jnp.dot(normed_first.T, d_value, preferred_element_type=jnp.float32)
    d_normed_first = jnp.dot(d_query, w_query.T, preferred_element_type=jnp.float32) + jnp.dot(d_key, w_key.T, preferred_element_type=jnp.float32) + jnp.dot(d_value, w_value.T, preferred_element_type=jnp.float32)
    d_gain_first, d_source = norm_backward(d_normed_first, source, inv_first, gain_first, d_middle)
    return (d_source, (d_query_w, d_key_w, d_value_w, d_out_w, d_gate_w, d_up_w, d_down, d_gain_first, d_gain_second))

def reference(hidden_in, out_grad, block_pos, norm1_gain, norm2_gain, wq, wk, wv, wo, w_gate, w_up, w_down):

    def section_weights(layer):
        return (norm1_gain[layer], norm2_gain[layer], wq[layer], wk[layer], wv[layer], wo[layer], w_gate[layer], w_up[layer], w_down[layer])
    first_weights = section_weights(0)
    second_weights = section_weights(1)
    grad_shapes = (wq.shape[1:], wk.shape[1:], wv.shape[1:], wo.shape[1:], w_gate.shape[1:], w_up.shape[1:], w_down.shape[1:], norm1_gain.shape[1:], norm2_gain.shape[1:])
    zero_first = tuple((jnp.zeros(shape_now, jnp.float32) for shape_now in grad_shapes))
    zero_second = tuple((jnp.zeros(shape_now, jnp.float32) for shape_now in grad_shapes))

    def per_micro(carry_grads, inputs_now):
        seq_input, seq_grad, block_row = inputs_now
        positions = positions_for(block_row, SEQ, BLK)
        middle_out, saved_first = block_forward(seq_input.astype(jnp.float32), positions, first_weights)
        final_out, saved_second = block_forward(middle_out, positions, second_weights)
        d_middle, grads_second = block_backward(seq_grad.astype(jnp.float32), saved_second, positions, second_weights)
        d_input, grads_first = block_backward(d_middle, saved_first, positions, first_weights)
        new_first = tuple((old_term + new_term for old_term, new_term in zip(carry_grads[0], grads_first)))
        new_second = tuple((old_term + new_term for old_term, new_term in zip(carry_grads[1], grads_second)))
        return ((new_first, new_second), (final_out.astype(jnp.bfloat16), d_input))
    totals, outputs_all = lax.scan(per_micro, (zero_first, zero_second), (hidden_in, out_grad, block_pos))
    stacked = tuple((jnp.stack([first_term, second_term]) for first_term, second_term in zip(totals[0], totals[1])))
    return (outputs_all[0], outputs_all[1], stacked[0], stacked[1], stacked[2], stacked[3], stacked[4], stacked[5], stacked[6], stacked[7], stacked[8])
```

```python
import math

import jax
import jax.numpy as jnp
from jax import lax
from jax.sharding import PartitionSpec as P

EPS = 1e-06
ROPE_LOG = math.log(10000.0)
NEG_FILL = -1e30
LANES = 128
STREAMS = 1
BF = jnp.bfloat16
F32 = jnp.float32


def shift(value, axis, steps, group=None):
    count = lax.axis_size(axis)
    group = count if group is None else group
    pairs = [(i, i // group * group + (i % group + steps) % group) for i in range(count)]
    return lax.ppermute(value, axis, pairs)


def mm(a, b):
    return jnp.dot(a, b, preferred_element_type=F32)


def mm_nt(a, b):
    return lax.dot_general(a, b, (((1,), (1,)), ((), ())), preferred_element_type=F32)


def mm_tn(a, b):
    return lax.dot_general(a, b, (((0,), (0,)), ((), ())), preferred_element_type=F32)


def pick(index, options):
    result = options[0]
    for number in range(1, len(options)):
        result = jnp.where(index == number, options[number], result)
    return result


def gather_parts(value, axis):
    count = lax.axis_size(axis)
    me = lax.axis_index(axis)
    parts = [value] + [shift(value, axis, s) for s in range(1, count)]
    return [pick((me - place) % count, parts) for place in range(count)]


def gather_cols(value, axis):
    return jnp.concatenate(gather_parts(value, axis), axis=1)


def gather_rows(value, axis):
    count = lax.axis_size(axis)
    me = lax.axis_index(axis)
    rows = value.shape[0]
    full = jnp.zeros((count * rows, value.shape[1]), value.dtype)
    for s in range(count):
        part = value if s == 0 else shift(value, axis, s)
        full = lax.dynamic_update_slice_in_dim(full, part, (me - s) % count * rows, 0)
    return full


def reduce_rows(value, axis):
    count = lax.axis_size(axis)
    me = lax.axis_index(axis)
    rows = value.shape[0] // count
    total = lax.dynamic_slice_in_dim(value, me * rows, rows, 0).astype(F32)
    for s in range(1, count):
        block = lax.dynamic_slice_in_dim(value, (me + s) % count * rows, rows, 0)
        total = total + shift(block, axis, s).astype(F32)
    return total


def reduce_cols(value, axis):
    count = lax.axis_size(axis)
    me = lax.axis_index(axis)
    width = value.shape[1] // count
    blocks = [value[:, p * width : (p + 1) * width] for p in range(count)]
    total = pick(me, blocks).astype(F32)
    for s in range(1, count):
        total = total + shift(pick((me + s) % count, blocks), axis, s).astype(F32)
    return total


def sum_small(value, axis):
    total = value
    for s in range(1, lax.axis_size(axis)):
        total = total + shift(value, axis, s)
    return total


def split_two(value):
    high = lax.reduce_precision(value, 8, 7)
    return high, value - high


def side_columns(terms):
    rows = terms[0].shape[0]
    column = lax.broadcasted_iota(jnp.int32, (rows, LANES), 1)
    block = jnp.zeros((rows, LANES), F32)
    for number, term in enumerate(terms):
        high, low = split_two(term)
        block = jnp.where(column == 2 * number, high[:, None], block)
        block = jnp.where(column == 2 * number + 1, low[:, None], block)
    return block.astype(BF)


def rope(positions, head_size):
    half = head_size // 2
    freqs = jnp.exp(jnp.arange(half, dtype=F32) * (-2.0 * ROPE_LOG / head_size))
    angles = positions.astype(F32)[:, None] * freqs
    return jnp.cos(angles), jnp.sin(angles)


def rotate(values, cosine, sine):
    half = values.shape[-1] // 2
    first = values[..., :half]
    second = values[..., half:]
    return jnp.concatenate([first * cosine - second * sine, second * cosine + first * sine], axis=-1)


def gelu_tanh(values):
    return jax.nn.gelu(values, approximate=True)


class Layout:
    def __init__(self, block_pos, first_micro, micros, row_count):
        self.n_wt = lax.axis_size("wt")
        self.n_ctx = lax.axis_size("ctx")
        self.group = self.n_wt // micros
        wt = lax.axis_index("wt")
        ctx = lax.axis_index("ctx")
        self.rows = row_count // self.group
        block_row = lax.dynamic_index_in_dim(block_pos, first_micro + wt // self.group, 0, keepdims=False)
        block_len = row_count * self.n_ctx // block_pos.shape[1]
        mine = wt % self.group

        def positions(ctx_at, group_at):
            places = ctx_at * row_count + group_at * self.rows + jnp.arange(self.rows, dtype=jnp.int32)
            blocks = (places // block_len)[:, None] == jnp.arange(block_row.shape[0], dtype=jnp.int32)[None, :]
            return jnp.sum(jnp.where(blocks, block_row[None, :], 0), axis=1) * block_len + places % block_len

        self.query_pos = positions(ctx, mine)
        self.key_pos = jnp.concatenate(
            [
                positions((ctx - s) % self.n_ctx, (mine - j) % self.group)
                for s in range(self.n_ctx)
                for j in range(self.group)
            ]
        )

    def gather_keys(self, rows):
        near = jnp.concatenate([rows] + [shift(rows, "wt", j, self.group) for j in range(1, self.group)], axis=0)
        return jnp.concatenate([near] + [shift(near, "ctx", s) for s in range(1, self.n_ctx)], axis=0)

    def reduce_keys(self, rows):
        near_rows = self.rows * self.group
        near = rows[:near_rows].astype(F32)
        for s in range(1, self.n_ctx):
            near = near + shift(rows[s * near_rows : (s + 1) * near_rows].astype(BF), "ctx", -s).astype(F32)
        total = near[: self.rows]
        for j in range(1, self.group):
            block = near[j * self.rows : (j + 1) * self.rows].astype(BF)
            total = total + shift(block, "wt", -j, self.group).astype(F32)
        return total


def layer_forward(source, layout, params):
    gain_first, gain_second, w_proj, w_out, w_gate, w_up, w_down = params
    query_width = w_out.shape[0]
    head_size = (w_proj.shape[1] - query_width) // 2
    head_count = query_width // head_size
    width_all = source.shape[1] * layout.n_wt
    rows = layout.rows
    square = jnp.sum(source * source, axis=1)
    scaled = (source * gain_first).astype(BF)
    partial = jnp.concatenate([mm(scaled, w_proj).astype(BF), side_columns([square])], axis=1)
    total = reduce_rows(partial, "wt")
    proj_width = query_width + 2 * head_size
    square_all = total[:, proj_width] + total[:, proj_width + 1]
    inv_first = lax.rsqrt(square_all / width_all + EPS)
    projected = total[:, :proj_width] * inv_first[:, None]
    cosine, sine = rope(layout.query_pos, head_size)
    queries = rotate(
        projected[:, :query_width].reshape(rows, head_count, head_size), cosine[:, None], sine[:, None]
    ).astype(BF)
    key_rows = rotate(projected[:, query_width : query_width + head_size], cosine, sine).astype(BF)
    value_rows = projected[:, query_width + head_size :].astype(BF)
    pairs_all = layout.gather_keys(jnp.concatenate([key_rows, value_rows], axis=1))
    all_keys = pairs_all[:, :head_size]
    all_values = pairs_all[:, head_size:]
    query_rows = queries.reshape(rows * head_count, head_size)
    row_pos = jnp.repeat(layout.query_pos, head_count)
    raw = mm_nt(query_rows, all_keys) * head_size ** (-0.5)
    scores = jnp.where(layout.key_pos[None, :] <= row_pos[:, None], raw, NEG_FILL)
    row_max = jnp.max(scores, axis=1, keepdims=True)
    raised = jnp.exp(scores - row_max)
    log_total = row_max + jnp.log(jnp.sum(raised, axis=1, keepdims=True))
    probs = jnp.exp(scores - log_total)
    probs_low = probs.astype(BF)
    attended = mm(probs_low, all_values).astype(BF).reshape(rows, query_width)
    attended_full = gather_rows(attended, "wt")
    middle = source + mm(attended_full, w_out)
    middle_full = gather_cols(middle.astype(BF), "wt").astype(F32)
    inv_second = lax.rsqrt(jnp.sum(middle_full * middle_full, axis=1) / width_all + EPS)
    normed_second = (middle_full * inv_second[:, None] * gain_second).astype(BF)
    gate_pre = mm(normed_second, w_gate)
    up_pre = mm(normed_second, w_up)
    hidden_act = (gelu_tanh(gate_pre) * up_pre).astype(BF)
    update = reduce_cols(mm(hidden_act, w_down).astype(BF), "wt")
    saved = (
        source,
        inv_first,
        projected,
        query_rows,
        all_keys,
        all_values,
        probs,
        attended_full,
        middle,
        inv_second,
        normed_second,
        gate_pre,
        up_pre,
        hidden_act,
        cosine,
        sine,
    )
    return middle + update, saved


def layer_backward(grad_out, layout, saved, params):
    gain_first, gain_second, w_proj, w_out, w_gate, w_up, w_down = params
    (
        source,
        inv_first,
        projected,
        query_rows,
        all_keys,
        all_values,
        probs,
        attended_full,
        middle,
        inv_second,
        normed_second,
        gate_pre,
        up_pre,
        hidden_act,
        cosine,
        sine,
    ) = saved
    query_width = w_out.shape[0]
    proj_width = w_proj.shape[1]
    head_size = (proj_width - query_width) // 2
    head_count = query_width // head_size
    width_all = source.shape[1] * layout.n_wt
    rows = layout.rows
    score_scale = head_size ** (-0.5)
    grad_full = gather_cols(grad_out.astype(BF), "wt")
    d_hidden = mm_nt(grad_full, w_down)
    activated, pull_back = jax.vjp(gelu_tanh, gate_pre)
    d_gate = pull_back(d_hidden * up_pre)[0].astype(BF)
    d_up = (d_hidden * activated).astype(BF)
    inner_part = jnp.sum(d_gate.astype(F32) * gate_pre + d_up.astype(F32) * up_pre, axis=1)
    inner = sum_small(inner_part, "wt") / (inv_second * width_all)
    d_normed = reduce_cols((mm_nt(d_gate, w_gate) + mm_nt(d_up, w_up)).astype(BF), "wt")
    d_middle = (
        grad_out
        + inv_second[:, None] * d_normed * gain_second_local(gain_second, source.shape[1])
        - middle * (inv_second**3 * inner)[:, None]
    )
    d_gain_second = jnp.sum(d_normed * middle * inv_second[:, None], axis=0)
    d_middle_low = d_middle.astype(BF)
    d_attended = reduce_rows(mm_nt(d_middle_low, w_out).astype(BF), "wt").astype(BF)
    d_rows = d_attended.reshape(rows * head_count, head_size)
    probs_low = probs.astype(BF)
    d_values_all = mm_tn(probs_low, d_rows)
    d_probs = mm_nt(d_rows, all_values)
    delta = jnp.sum(probs * d_probs, axis=1, keepdims=True)
    d_scores = (probs * (d_probs - delta) * score_scale).astype(BF)
    d_query_rows = mm(d_scores, all_keys)
    d_keys_all = mm_tn(d_scores, query_rows)
    d_pairs = layout.reduce_keys(jnp.concatenate([d_keys_all, d_values_all], axis=1))
    d_query = rotate(
        d_query_rows.reshape(rows, head_count, head_size), cosine[:, None], -sine[:, None]
    ).reshape(rows, query_width)
    d_key = rotate(d_pairs[:, :head_size], cosine, -sine)
    d_projected = jnp.concatenate([d_query, d_key, d_pairs[:, head_size:]], axis=1).astype(BF)
    inner_own = jnp.sum(d_projected.astype(F32) * projected, axis=1) * inv_first * inv_first / width_all
    packed = gather_rows(jnp.concatenate([d_projected, side_columns([inv_first, inner_own])], axis=1), "wt")
    d_projected_full = packed[:, :proj_width]
    side = packed[:, proj_width : proj_width + 4].astype(F32)
    inv_full = side[:, 0:1] + side[:, 1:2]
    inner_full = side[:, 2:3] + side[:, 3:4]
    d_first = mm_nt(d_projected_full, w_proj)
    d_source = d_middle + inv_full * d_first * gain_first - source * inner_full
    d_gain_first = jnp.sum(d_first * source * inv_full, axis=0)
    normed_first = (source * inv_full * gain_first).astype(BF)
    terms = dict(
        act=hidden_act,
        grad=grad_full,
        normed=normed_second,
        d_gate=d_gate,
        d_up=d_up,
        attended=attended_full,
        d_middle=d_middle_low,
        first=normed_first,
        d_projected=d_projected_full,
    )
    return d_source, terms, d_gain_first, d_gain_second


def gain_second_local(gain_full, width):
    return lax.dynamic_slice_in_dim(gain_full, lax.axis_index("wt") * width, width, 0)


def both_sections(value):
    count = lax.axis_size("section")
    return jnp.concatenate([value] + [shift(value, "section", s) for s in range(1, count)], axis=0)


def both_halves(section_id, low, high):
    own = jnp.where(section_id == 0, low, high)
    other = jnp.where(section_id == 0, high, low)
    return jnp.concatenate([own, shift(other, "section", 1)], axis=0)


def halves(value):
    width = value.shape[1] // 2
    return value[:, :width], value[:, width:]


def by_owner(value, query_width, head_size, n_ctx):
    query_part = query_width // n_ctx
    head_part = head_size // n_ctx
    pieces = []
    for c in range(n_ctx):
        pieces.append(value[:, c * query_part : (c + 1) * query_part])
        for base in (query_width, query_width + head_size):
            pieces.append(value[:, base + c * head_part : base + (c + 1) * head_part])
    return jnp.concatenate(pieces, axis=1)


def weight_grads(section_id, terms, query_width, head_size):
    n_ctx = lax.axis_size("ctx")

    def keep(partial):
        return lax.psum_scatter(partial.astype(BF), "ctx", scatter_dimension=0, tiled=True)

    grad = both_sections(terms["grad"])
    down = keep(mm_tn(grad, both_halves(section_id, *halves(terms["act"]))))
    normed = both_sections(terms["normed"])
    gate_up = keep(mm_tn(normed, both_halves(section_id, terms["d_gate"], terms["d_up"])))
    attended = both_sections(terms["attended"])
    out = keep(mm_tn(attended, both_halves(section_id, *halves(terms["d_middle"]))))
    projected = both_sections(by_owner(terms["d_projected"], query_width, head_size, n_ctx))
    proj = keep(mm_tn(projected, both_halves(section_id, *halves(terms["first"]))))
    return down, gate_up, out, proj


def home(section_id, first_block, second_block):
    kept = jnp.where(section_id == 0, first_block, second_block)
    sent = jnp.where(section_id == 0, second_block, first_block)
    received = shift(sent, "section", 1)
    low = jnp.where(section_id == 0, kept, received)
    high = jnp.where(section_id == 0, received, kept)
    return low, high


def local(hidden_in, out_grad, block_pos, norm1_gain, norm2_gain, wq, wk, wv, wo, w_gate, w_up, w_down):
    n_section = lax.axis_size("section")
    assert n_section == 2
    n_ctx = lax.axis_size("ctx")
    section_id = lax.axis_index("section")
    micro_count, row_count, width = hidden_in.shape
    micro_own = micro_count // n_section
    query_width = wq.shape[2]
    head_size = wk.shape[2]

    def fetch(weight):
        return lax.all_gather(weight, "section", axis=0, tiled=False)

    w_proj = fetch(jnp.concatenate([wq[0], wk[0], wv[0]], axis=1))
    weights = [w_proj] + [fetch(w[0]) for w in (wo, w_gate, w_up, w_down)]
    gains = jnp.concatenate([norm1_gain, norm2_gain], axis=0)
    other_gains = shift(gains, "section", 1)
    gains = jnp.concatenate(
        [jnp.where(section_id == 0, gains, other_gains), jnp.where(section_id == 0, other_gains, gains)], axis=0
    )
    gains_full = gather_cols(gains, "wt")
    params = [
        (gains[2 * l], gains_full[2 * l + 1]) + tuple(w[l] for w in weights) for l in range(n_section)
    ]
    first_micro = section_id * micro_own
    micros = micro_own // STREAMS
    hidden = lax.dynamic_slice_in_dim(hidden_in, first_micro, micro_own, 0)
    cotangent = lax.dynamic_slice_in_dim(out_grad, first_micro, micro_own, 0)
    layouts = [Layout(block_pos, first_micro + k * micros, micros, row_count) for k in range(STREAMS)]

    def rows_of(value, k):
        return value[k * micros : (k + 1) * micros].reshape(micros * row_count, width).astype(F32)

    states = [rows_of(hidden, k) for k in range(STREAMS)]
    saved = []
    for l in range(n_section):
        results = [layer_forward(states[k], layouts[k], params[l]) for k in range(STREAMS)]
        states = [result[0] for result in results]
        saved.append([result[1] for result in results])
    out_own = jnp.concatenate([state.astype(BF) for state in states], axis=0)
    grads = [rows_of(cotangent, k) for k in range(STREAMS)]
    blocks = {}
    gain_grads = {}
    for l in reversed(range(n_section)):
        results = [layer_backward(grads[k], layouts[k], saved[l][k], params[l]) for k in range(STREAMS)]
        grads = [result[0] for result in results]
        terms = {
            name: jnp.concatenate([result[1][name] for result in results], axis=0) for name in results[0][1]
        }
        blocks[l] = weight_grads(section_id, terms, query_width, head_size)
        gain_grads[l] = jnp.stack([sum(r[2] for r in results), sum(r[3] for r in results)])
    in_grad_own = jnp.concatenate(grads, axis=0)

    def everywhere(own):
        low, high = own, shift(own, "section", 1)
        both = jnp.concatenate(
            [jnp.where(section_id == 0, low, high), jnp.where(section_id == 0, high, low)], axis=0
        )
        return both.reshape(micro_count, row_count, width)

    out = everywhere(out_own)
    in_grad = everywhere(in_grad_own)
    gain_sum = lax.psum(jnp.stack([gain_grads[0], gain_grads[1]]), ("section", "ctx"))
    gain_mine = jnp.where(section_id == 0, gain_sum[0], gain_sum[1])
    down, gate_up, out_w, proj = (home(section_id, a, b) for a, b in zip(blocks[0], blocks[1]))
    grad_down = jnp.concatenate(down, axis=1).T.astype(F32)
    grad_gate, grad_up = (half.astype(F32) for half in gate_up)
    grad_wo = jnp.concatenate(out_w, axis=1).astype(F32)
    grad_proj = jnp.concatenate(proj, axis=1).T.astype(F32)
    query_part = query_width // n_ctx
    head_part = head_size // n_ctx
    return (
        out,
        in_grad,
        grad_proj[:, :query_part][None],
        grad_proj[:, query_part : query_part + head_part][None],
        grad_proj[:, query_part + head_part :][None],
        grad_wo[None],
        grad_gate[None],
        grad_up[None],
        grad_down[None],
        gain_mine[0][None],
        gain_mine[1][None],
    )


def solution(mesh):
    return jax.shard_map(
        local,
        mesh=mesh,
        in_specs=(
            P(None, "ctx", "wt"),
            P(None, "ctx", "wt"),
            P(),
            P("section", "wt"),
            P("section", "wt"),
            P("section", "wt", None),
            P("section", "wt", None),
            P("section", "wt", None),
            P("section", None, "wt"),
            P("section", None, "wt"),
            P("section", None, "wt"),
            P("section", "wt", None),
        ),
        out_specs=(
            P(None, "ctx", "wt"),
            P(None, "ctx", "wt"),
            P("section", "wt", "ctx"),
            P("section", "wt", "ctx"),
            P("section", "wt", "ctx"),
            P("section", "ctx", "wt"),
            P("section", "ctx", "wt"),
            P("section", "ctx", "wt"),
            P("section", "wt", "ctx"),
            P("section", "wt"),
            P("section", "wt"),
        ),
        check_vma=False,
    )
```

```python
import math

import jax
import jax.numpy as jnp
from jax import lax
from jax.experimental.layout import Layout as ArrayLayout, with_layout_constraint
from jax.sharding import PartitionSpec as P

EPS = 1e-06
ROPE_LOG = math.log(10000.0)
NEG_FILL = -1e30
LANES = 128
BF = jnp.bfloat16
F32 = jnp.float32


def shift(value, axis, steps, group=None):
    count = lax.axis_size(axis)
    group = count if group is None else group
    pairs = [(i, i // group * group + (i % group + steps) % group) for i in range(count)]
    return lax.ppermute(value, axis, pairs)


def natural(value):
    return with_layout_constraint(value, ArrayLayout(major_to_minor=tuple(range(value.ndim))))


def after(values, fillers):
    if not fillers:
        return list(values)
    held = lax.optimization_barrier(tuple(values) + tuple(fillers))
    return list(held[: len(values)])


def mm(a, b):
    return jnp.dot(a, b, preferred_element_type=F32)


def mm_nt(a, b):
    return lax.dot_general(a, b, (((1,), (1,)), ((), ())), preferred_element_type=F32)


def mm_tn(a, b):
    return lax.dot_general(a, b, (((0,), (0,)), ((), ())), preferred_element_type=F32)


def pick(index, options):
    result = options[0]
    for number in range(1, len(options)):
        result = jnp.where(index == number, options[number], result)
    return result


def gather_cols(value, axis, fillers=()):
    count = lax.axis_size(axis)
    me = lax.axis_index(axis)
    parts = [value] + after([shift(value, axis, s) for s in range(1, count)], fillers)
    return natural(jnp.concatenate([pick((me - place) % count, parts) for place in range(count)], axis=1))


def gather_rows(value, axis, fillers=()):
    count = lax.axis_size(axis)
    me = lax.axis_index(axis)
    rows = value.shape[0]
    full = jnp.zeros((count * rows, value.shape[1]), value.dtype)
    parts = [value] + after([shift(value, axis, s) for s in range(1, count)], fillers)
    for s in range(count):
        full = lax.dynamic_update_slice_in_dim(full, parts[s], (me - s) % count * rows, 0)
    return natural(full)


def reduce_rows(value, axis, fillers=()):
    count = lax.axis_size(axis)
    me = lax.axis_index(axis)
    rows = value.shape[0] // count
    blocks = [lax.dynamic_slice_in_dim(value, (me + s) % count * rows, rows, 0) for s in range(count)]
    received = after([shift(blocks[s], axis, s) for s in range(1, count)], fillers)
    return sum((part.astype(F32) for part in received), blocks[0].astype(F32))


def reduce_cols(value, axis, fillers=()):
    count = lax.axis_size(axis)
    me = lax.axis_index(axis)
    width = value.shape[1] // count
    blocks = [value[:, p * width : (p + 1) * width] for p in range(count)]
    chosen = [pick((me + s) % count, blocks) for s in range(count)]
    received = after([shift(chosen[s], axis, s) for s in range(1, count)], fillers)
    return sum((part.astype(F32) for part in received), chosen[0].astype(F32))


def sum_small(value, axis):
    total = value
    for s in range(1, lax.axis_size(axis)):
        total = total + shift(value, axis, s)
    return total


def split_two(value):
    high = lax.reduce_precision(value, 8, 7)
    return high, value - high


def side_columns(terms):
    rows = terms[0].shape[0]
    column = lax.broadcasted_iota(jnp.int32, (rows, LANES), 1)
    block = jnp.zeros((rows, LANES), F32)
    for number, term in enumerate(terms):
        high, low = split_two(term)
        block = jnp.where(column == 2 * number, high[:, None], block)
        block = jnp.where(column == 2 * number + 1, low[:, None], block)
    return block.astype(BF)


def rope(positions, head_size):
    half = head_size // 2
    freqs = jnp.exp(jnp.arange(half, dtype=F32) * (-2.0 * ROPE_LOG / head_size))
    angles = positions.astype(F32)[:, None] * freqs
    return jnp.cos(angles), jnp.sin(angles)


def rotate(values, cosine, sine):
    half = values.shape[-1] // 2
    first = values[..., :half]
    second = values[..., half:]
    return jnp.concatenate([first * cosine - second * sine, second * cosine + first * sine], axis=-1)


def gelu_tanh(values):
    return jax.nn.gelu(values, approximate=True)


class Layout:
    def __init__(self, block_pos, first_micro, micros, row_count):
        self.n_wt = lax.axis_size("wt")
        self.n_ctx = lax.axis_size("ctx")
        self.group = self.n_wt // micros
        wt = lax.axis_index("wt")
        ctx = lax.axis_index("ctx")
        self.rows = row_count // self.group
        block_row = lax.dynamic_index_in_dim(block_pos, first_micro + wt // self.group, 0, keepdims=False)
        block_len = row_count * self.n_ctx // block_pos.shape[1]
        mine = wt % self.group

        def positions(ctx_at, group_at):
            places = ctx_at * row_count + group_at * self.rows + jnp.arange(self.rows, dtype=jnp.int32)
            blocks = (places // block_len)[:, None] == jnp.arange(block_row.shape[0], dtype=jnp.int32)[None, :]
            return jnp.sum(jnp.where(blocks, block_row[None, :], 0), axis=1) * block_len + places % block_len

        self.query_pos = positions(ctx, mine)
        self.key_pos = jnp.concatenate(
            [
                positions((ctx - s) % self.n_ctx, (mine - j) % self.group)
                for s in range(self.n_ctx)
                for j in range(self.group)
            ]
        )

    def gather_keys(self, rows):
        near = jnp.concatenate([rows] + [shift(rows, "wt", j, self.group) for j in range(1, self.group)], axis=0)
        return jnp.concatenate([near] + [shift(near, "ctx", s) for s in range(1, self.n_ctx)], axis=0)

    def reduce_keys(self, rows):
        near_rows = self.rows * self.group
        near = rows[:near_rows].astype(F32)
        for s in range(1, self.n_ctx):
            near = near + shift(rows[s * near_rows : (s + 1) * near_rows].astype(BF), "ctx", -s).astype(F32)
        total = near[: self.rows]
        for j in range(1, self.group):
            block = near[j * self.rows : (j + 1) * self.rows].astype(BF)
            total = total + shift(block, "wt", -j, self.group).astype(F32)
        return total


def layer_forward(source, layout, params, early=None):
    gain_first, gain_second, w_proj, w_out, w_gate, w_up, w_down = params
    query_width = w_out.shape[0]
    head_size = (w_proj.shape[1] - query_width) // 2
    head_count = query_width // head_size
    width_all = source.shape[1] * layout.n_wt
    rows = layout.rows
    square = jnp.sum(source * source, axis=1)
    scaled = (source * gain_first).astype(BF)
    partial = jnp.concatenate([mm(scaled, w_proj).astype(BF), side_columns([square])], axis=1)
    total = reduce_rows(partial, "wt")
    proj_width = query_width + 2 * head_size
    square_all = total[:, proj_width] + total[:, proj_width + 1]
    inv_first = lax.rsqrt(square_all / width_all + EPS)
    projected = total[:, :proj_width] * inv_first[:, None]
    cosine, sine = rope(layout.query_pos, head_size)
    queries = rotate(
        projected[:, :query_width].reshape(rows, head_count, head_size), cosine[:, None], sine[:, None]
    ).astype(BF)
    key_rows = rotate(projected[:, query_width : query_width + head_size], cosine, sine).astype(BF)
    value_rows = projected[:, query_width + head_size :].astype(BF)
    pairs_all = layout.gather_keys(jnp.concatenate([key_rows, value_rows], axis=1))
    all_keys = pairs_all[:, :head_size]
    all_values = pairs_all[:, head_size:]
    query_rows = queries.reshape(rows * head_count, head_size)
    row_pos = jnp.repeat(layout.query_pos, head_count)
    raw = mm_nt(query_rows, all_keys) * head_size ** (-0.5)
    scores = jnp.where(layout.key_pos[None, :] <= row_pos[:, None], raw, NEG_FILL)
    row_max = jnp.max(scores, axis=1, keepdims=True)
    raised = jnp.exp(scores - row_max)
    log_total = row_max + jnp.log(jnp.sum(raised, axis=1, keepdims=True))
    probs = jnp.exp(scores - log_total)
    probs_low = probs.astype(BF)
    attended = mm(probs_low, all_values).astype(BF).reshape(rows, query_width)
    attended_full = gather_rows(attended, "wt")
    middle = source + mm(attended_full, w_out)
    middle_full = gather_cols(middle.astype(BF), "wt")
    if early is not None:
        middle_full, early = lax.optimization_barrier((middle_full, early))
        early = gather_cols(early, "wt")
    middle_full = middle_full.astype(F32)
    inv_second = lax.rsqrt(jnp.sum(middle_full * middle_full, axis=1) / width_all + EPS)
    normed_second = (middle_full * inv_second[:, None] * gain_second).astype(BF)
    gate_pre = mm(normed_second, w_gate)
    up_pre = mm(normed_second, w_up)
    hidden_act = (gelu_tanh(gate_pre) * up_pre).astype(BF)
    update = reduce_cols(mm(hidden_act, w_down).astype(BF), "wt")
    saved = (
        source,
        inv_first,
        projected,
        query_rows,
        all_keys,
        all_values,
        probs,
        attended_full,
        middle,
        inv_second,
        normed_second,
        gate_pre,
        up_pre,
        hidden_act,
        cosine,
        sine,
    )
    return middle + update, saved, early


def layer_backward(grad_out, grad_full, layout, saved, params, pending, merge):
    gain_first, gain_second, w_proj, w_out, w_gate, w_up, w_down = params
    (
        source,
        inv_first,
        projected,
        query_rows,
        all_keys,
        all_values,
        probs,
        attended_full,
        middle,
        inv_second,
        normed_second,
        gate_pre,
        up_pre,
        hidden_act,
        cosine,
        sine,
    ) = saved
    section_id = lax.axis_index("section")
    n_ctx = layout.n_ctx
    query_width = w_out.shape[0]
    proj_width = w_proj.shape[1]
    head_size = (proj_width - query_width) // 2
    head_count = query_width // head_size
    width_all = source.shape[1] * layout.n_wt
    rows = layout.rows
    score_scale = head_size ** (-0.5)
    pending_grads = pending() if pending else []
    if grad_full is None:
        grad_full = gather_cols(grad_out.astype(BF), "wt", pending_grads)
    pending_kept = keep(*pending_grads) if pending_grads else None
    down = weight_grad(
        both_halves(section_id, *row_halves(grad_full, n_ctx)), both_sections(hidden_act)
    )
    if not merge:
        down_kept = keep(down)
        (grad_full,) = after([grad_full], [down])
    d_hidden = mm_nt(grad_full, w_down)
    activated, pull_back = jax.vjp(gelu_tanh, gate_pre)
    d_gate = pull_back(d_hidden * up_pre)[0].astype(BF)
    d_up = (d_hidden * activated).astype(BF)
    inner_part = jnp.sum(d_gate.astype(F32) * gate_pre + d_up.astype(F32) * up_pre, axis=1)
    inner = sum_small(inner_part, "wt") / (inv_second * width_all)
    gate_up = weight_grad(both_sections(normed_second), both_halves(section_id, d_gate, d_up))
    feed_kept = keep(down, gate_up) if merge else (down_kept, keep(gate_up))
    d_normed = reduce_cols(
        (mm_nt(d_gate, w_gate) + mm_nt(d_up, w_up)).astype(BF), "wt", [down, gate_up] if merge else [gate_up]
    )
    gain_local = lax.dynamic_slice_in_dim(gain_second, lax.axis_index("wt") * source.shape[1], source.shape[1], 0)
    d_middle = (
        grad_out
        + inv_second[:, None] * d_normed * gain_local
        - middle * (inv_second**3 * inner)[:, None]
    )
    d_gain_second = jnp.sum(d_normed * middle * inv_second[:, None], axis=0)
    d_middle_low = d_middle.astype(BF)
    out_grad = weight_grad(
        both_halves(section_id, *row_halves(attended_full, n_ctx)), both_sections(d_middle_low)
    )
    d_attended = reduce_rows(mm_nt(d_middle_low, w_out).astype(BF), "wt", [out_grad]).astype(BF)
    d_rows = d_attended.reshape(rows * head_count, head_size)
    probs_low = probs.astype(BF)
    d_values_all = mm_tn(probs_low, d_rows)
    d_probs = mm_nt(d_rows, all_values)
    delta = jnp.sum(probs * d_probs, axis=1, keepdims=True)
    d_scores = (probs * (d_probs - delta) * score_scale).astype(BF)
    d_query_rows = mm(d_scores, all_keys)
    d_keys_all = mm_tn(d_scores, query_rows)
    d_pairs = layout.reduce_keys(jnp.concatenate([d_keys_all, d_values_all], axis=1))
    d_query = rotate(
        d_query_rows.reshape(rows, head_count, head_size), cosine[:, None], -sine[:, None]
    ).reshape(rows, query_width)
    d_key = rotate(d_pairs[:, :head_size], cosine, -sine)
    d_projected = jnp.concatenate([d_query, d_key, d_pairs[:, head_size:]], axis=1).astype(BF)
    inner_own = jnp.sum(d_projected.astype(F32) * projected, axis=1) * inv_first * inv_first / width_all
    packed = gather_rows(jnp.concatenate([d_projected, side_columns([inv_first, inner_own])], axis=1), "wt")
    d_projected_full = packed[:, :proj_width]
    side = packed[:, proj_width : proj_width + 4].astype(F32)
    inv_full = side[:, 0:1] + side[:, 1:2]
    inner_full = side[:, 2:3] + side[:, 3:4]
    d_first = mm_nt(d_projected_full, w_proj)
    d_source = d_middle + inv_full * d_first * gain_first - source * inner_full
    d_gain_first = jnp.sum(d_first * source * inv_full, axis=0)
    normed_first = (source * inv_full * gain_first).astype(BF)

    def attention_grads():
        owned = by_owner(d_projected_full, query_width, head_size, n_ctx)
        proj_grad = weight_grad(
            both_halves(section_id, *row_halves(owned, n_ctx)), both_sections(normed_first)
        )
        return [out_grad, proj_grad]

    return d_source, feed_kept, attention_grads, pending_kept, d_gain_first, d_gain_second


def both_sections(value):
    return jnp.concatenate([value, shift(value, "section", 1)], axis=0)


def both_halves(section_id, low, high):
    own = jnp.where(section_id == 0, low, high)
    other = jnp.where(section_id == 0, high, low)
    return jnp.concatenate([own, shift(other, "section", 1)], axis=0)


def row_halves(value, n_ctx):
    part = value.shape[1] // n_ctx
    half = part // 2
    return tuple(
        jnp.concatenate([value[:, c * part + h * half : c * part + (h + 1) * half] for c in range(n_ctx)], axis=1)
        for h in range(2)
    )


def by_owner(value, query_width, head_size, n_ctx):
    query_part = query_width // n_ctx
    head_part = head_size // n_ctx
    pieces = []
    for c in range(n_ctx):
        pieces.append(value[:, c * query_part : (c + 1) * query_part])
        for base in (query_width, query_width + head_size):
            pieces.append(value[:, base + c * head_part : base + (c + 1) * head_part])
    return jnp.concatenate(pieces, axis=1)


def weight_grad(left, right):
    return natural(mm_tn(left, right).astype(BF))


def keep(*partials):
    n_ctx = lax.axis_size("ctx")
    heights = [partial.shape[0] // n_ctx for partial in partials]
    width = partials[0].shape[1]
    joined = partials[0]
    if len(partials) > 1:
        blocks = [partial.reshape(n_ctx, height, width) for partial, height in zip(partials, heights)]
        joined = jnp.concatenate(blocks, axis=1).reshape(n_ctx * sum(heights), width)
    mine = lax.psum_scatter(joined, "ctx", scatter_dimension=0, tiled=True)
    if len(partials) == 1:
        return mine
    ends = [sum(heights[: k + 1]) for k in range(len(heights))]
    return tuple(mine[end - height : end] for end, height in zip(ends, heights))


def home(section_id, first_block, second_block):
    kept = jnp.where(section_id == 0, first_block, second_block)
    sent = jnp.where(section_id == 0, second_block, first_block)
    received = shift(sent, "section", 1)
    low = jnp.where(section_id == 0, kept, received)
    high = jnp.where(section_id == 0, received, kept)
    return low, high


def local(hidden_in, out_grad, block_pos, norm1_gain, norm2_gain, wq, wk, wv, wo, w_gate, w_up, w_down):
    n_section = lax.axis_size("section")
    assert n_section == 2
    n_ctx = lax.axis_size("ctx")
    section_id = lax.axis_index("section")
    micro_count, row_count, width = hidden_in.shape
    micro_own = micro_count // n_section
    query_width = wq.shape[2]
    head_size = wk.shape[2]

    def fetch(weight):
        return lax.all_gather(weight, "section", axis=0, tiled=False)

    def fetch_fast(weight):
        received = shift(weight, "section", 1)
        return lax.optimization_barrier(
            (jnp.where(section_id == 0, weight, received), jnp.where(section_id == 0, received, weight))
        )

    w_proj = fetch_fast(jnp.concatenate([wq[0], wk[0], wv[0]], axis=1))
    weights = (w_proj, fetch(wo[0]), fetch(w_gate[0]), fetch(w_up[0]), fetch_fast(w_down[0]))
    gains = jnp.concatenate([norm1_gain, norm2_gain], axis=0)
    other_gains = shift(gains, "section", 1)
    gains = jnp.concatenate(
        [jnp.where(section_id == 0, gains, other_gains), jnp.where(section_id == 0, other_gains, gains)], axis=0
    )
    gains_full = gather_cols(gains, "wt")
    params = [
        (gains[2 * l], gains_full[2 * l + 1]) + tuple(w[l] for w in weights) for l in range(n_section)
    ]
    first_micro = section_id * micro_own
    layout = Layout(block_pos, first_micro, micro_own, row_count)

    def own_rows(value):
        return lax.dynamic_slice_in_dim(value, first_micro, micro_own, 0).reshape(micro_own * row_count, width)

    cotangent = own_rows(out_grad)
    state, saved_0, grad_full = layer_forward(own_rows(hidden_in).astype(F32), layout, params[0], cotangent)
    state, saved_1, _ = layer_forward(state, layout, params[1])
    out_own = state.astype(BF)
    grad, feed_1, pending, _, d_first_1, d_second_1 = layer_backward(
        cotangent.astype(F32), grad_full, layout, saved_1, params[1], None, False
    )
    in_grad_own, feed_0, pending, attention_1, d_first_0, d_second_0 = layer_backward(
        grad, None, layout, saved_0, params[0], pending, True
    )
    attention_0 = keep(*pending())

    def everywhere(own):
        low, high = own, shift(own, "section", 1)
        both = jnp.concatenate(
            [jnp.where(section_id == 0, low, high), jnp.where(section_id == 0, high, low)], axis=0
        )
        return both.reshape(micro_count, row_count, width)

    out = everywhere(out_own)
    in_grad = everywhere(in_grad_own)
    gain_sum = lax.psum(
        jnp.stack([jnp.stack([d_first_0, d_second_0]), jnp.stack([d_first_1, d_second_1])]), ("section", "ctx")
    )
    gain_mine = jnp.where(section_id == 0, gain_sum[0], gain_sum[1])
    down, gate_up = (home(section_id, a, b) for a, b in zip(feed_0, feed_1))
    out_w, proj = (home(section_id, a, b) for a, b in zip(attention_0, attention_1))
    grad_down = jnp.concatenate(down, axis=0).T.astype(F32)
    grad_gate, grad_up = (half.astype(F32) for half in gate_up)
    grad_wo = jnp.concatenate(out_w, axis=0).astype(F32)
    grad_proj = jnp.concatenate(proj, axis=0).T.astype(F32)
    query_part = query_width // n_ctx
    head_part = head_size // n_ctx
    return (
        out,
        in_grad,
        grad_proj[:, :query_part][None],
        grad_proj[:, query_part : query_part + head_part][None],
        grad_proj[:, query_part + head_part :][None],
        grad_wo[None],
        grad_gate[None],
        grad_up[None],
        grad_down[None],
        gain_mine[0][None],
        gain_mine[1][None],
    )


def solution(mesh):
    return jax.shard_map(
        local,
        mesh=mesh,
        in_specs=(
            P(None, "ctx", "wt"),
            P(None, "ctx", "wt"),
            P(),
            P("section", "wt"),
            P("section", "wt"),
            P("section", "wt", None),
            P("section", "wt", None),
            P("section", "wt", None),
            P("section", None, "wt"),
            P("section", None, "wt"),
            P("section", None, "wt"),
            P("section", "wt", None),
        ),
        out_specs=(
            P(None, "ctx", "wt"),
            P(None, "ctx", "wt"),
            P("section", "wt", "ctx"),
            P("section", "wt", "ctx"),
            P("section", "wt", "ctx"),
            P("section", "ctx", "wt"),
            P("section", "ctx", "wt"),
            P("section", "ctx", "wt"),
            P("section", "wt", "ctx"),
            P("section", "wt"),
            P("section", "wt"),
        ),
        check_vma=False,
    )
```

```python
import math

import jax
import jax.numpy as jnp
from jax import lax
from jax.experimental.layout import Layout as ArrayLayout, with_layout_constraint
from jax.sharding import PartitionSpec as P

EPS = 1e-06
ROPE_LOG = math.log(10000.0)
NEG_FILL = -1e30
LANES = 128
BF = jnp.bfloat16
F32 = jnp.float32


def shift(value, axis, steps, group=None):
    count = lax.axis_size(axis)
    group = count if group is None else group
    pairs = [(i, i // group * group + (i % group + steps) % group) for i in range(count)]
    return lax.ppermute(value, axis, pairs)


def natural(value):
    return with_layout_constraint(value, ArrayLayout(major_to_minor=tuple(range(value.ndim))))


def after(values, fillers):
    if not fillers:
        return list(values)
    held = lax.optimization_barrier(tuple(values) + tuple(fillers))
    return list(held[: len(values)])


def mm(a, b):
    return jnp.dot(a, b, preferred_element_type=F32)


def mm_nt(a, b):
    return lax.dot_general(a, b, (((1,), (1,)), ((), ())), preferred_element_type=F32)


def mm_tn(a, b):
    return lax.dot_general(a, b, (((0,), (0,)), ((), ())), preferred_element_type=F32)


def pick(index, options):
    result = options[0]
    for number in range(1, len(options)):
        result = jnp.where(index == number, options[number], result)
    return result


def gather_cols(value, axis, fillers=()):
    count = lax.axis_size(axis)
    return join_cols([value] + after([shift(value, axis, s) for s in range(1, count)], fillers), axis)


def join_cols(parts, axis):
    me = lax.axis_index(axis)
    count = len(parts)
    return natural(jnp.concatenate([pick((me - place) % count, parts) for place in range(count)], axis=1))


def gather_rows(value, axis, fillers=()):
    count = lax.axis_size(axis)
    me = lax.axis_index(axis)
    rows = value.shape[0]
    full = jnp.zeros((count * rows, value.shape[1]), value.dtype)
    parts = [value] + after([shift(value, axis, s) for s in range(1, count)], fillers)
    for s in range(count):
        full = lax.dynamic_update_slice_in_dim(full, parts[s], (me - s) % count * rows, 0)
    return natural(full)


def reduce_rows(value, axis, fillers=()):
    count = lax.axis_size(axis)
    me = lax.axis_index(axis)
    rows = value.shape[0] // count
    blocks = [lax.dynamic_slice_in_dim(value, (me + s) % count * rows, rows, 0) for s in range(count)]
    received = after([shift(blocks[s], axis, s) for s in range(1, count)], fillers)
    return sum((part.astype(F32) for part in received), blocks[0].astype(F32))


def reduce_cols(value, axis, fillers=()):
    count = lax.axis_size(axis)
    me = lax.axis_index(axis)
    width = value.shape[1] // count
    blocks = [value[:, p * width : (p + 1) * width] for p in range(count)]
    chosen = [pick((me + s) % count, blocks) for s in range(count)]
    received = after([shift(chosen[s], axis, s) for s in range(1, count)], fillers)
    return sum((part.astype(F32) for part in received), chosen[0].astype(F32))


def sum_small(value, axis):
    total = value
    for s in range(1, lax.axis_size(axis)):
        total = total + shift(value, axis, s)
    return total


def split_two(value):
    high = lax.reduce_precision(value, 8, 7)
    return high, value - high


def side_columns(terms):
    rows = terms[0].shape[0]
    column = lax.broadcasted_iota(jnp.int32, (rows, LANES), 1)
    block = jnp.zeros((rows, LANES), F32)
    for number, term in enumerate(terms):
        high, low = split_two(term)
        block = jnp.where(column == 2 * number, high[:, None], block)
        block = jnp.where(column == 2 * number + 1, low[:, None], block)
    return block.astype(BF)


def rope(positions, head_size):
    half = head_size // 2
    freqs = jnp.exp(jnp.arange(half, dtype=F32) * (-2.0 * ROPE_LOG / head_size))
    angles = positions.astype(F32)[:, None] * freqs
    return jnp.cos(angles), jnp.sin(angles)


def rotate(values, cosine, sine):
    half = values.shape[-1] // 2
    first = values[..., :half]
    second = values[..., half:]
    return jnp.concatenate([first * cosine - second * sine, second * cosine + first * sine], axis=-1)


def gelu_tanh(values):
    return jax.nn.gelu(values, approximate=True)


class Layout:
    def __init__(self, block_pos, first_micro, micros, row_count):
        self.n_wt = lax.axis_size("wt")
        self.n_ctx = lax.axis_size("ctx")
        self.group = self.n_wt // micros
        wt = lax.axis_index("wt")
        ctx = lax.axis_index("ctx")
        self.rows = row_count // self.group
        block_row = lax.dynamic_index_in_dim(block_pos, first_micro + wt // self.group, 0, keepdims=False)
        block_len = row_count * self.n_ctx // block_pos.shape[1]
        mine = wt % self.group

        def positions(ctx_at, group_at):
            places = ctx_at * row_count + group_at * self.rows + jnp.arange(self.rows, dtype=jnp.int32)
            blocks = (places // block_len)[:, None] == jnp.arange(block_row.shape[0], dtype=jnp.int32)[None, :]
            return jnp.sum(jnp.where(blocks, block_row[None, :], 0), axis=1) * block_len + places % block_len

        self.query_pos = positions(ctx, mine)
        self.key_pos = jnp.concatenate(
            [
                positions((ctx - s) % self.n_ctx, (mine - j) % self.group)
                for s in range(self.n_ctx)
                for j in range(self.group)
            ]
        )

    def gather_keys(self, rows):
        near = jnp.concatenate([rows] + [shift(rows, "wt", j, self.group) for j in range(1, self.group)], axis=0)
        return jnp.concatenate([near] + [shift(near, "ctx", s) for s in range(1, self.n_ctx)], axis=0)

    def reduce_keys(self, rows):
        near_rows = self.rows * self.group
        near = rows[:near_rows].astype(F32)
        for s in range(1, self.n_ctx):
            near = near + shift(rows[s * near_rows : (s + 1) * near_rows].astype(BF), "ctx", -s).astype(F32)
        total = near[: self.rows]
        for j in range(1, self.group):
            block = near[j * self.rows : (j + 1) * self.rows].astype(BF)
            total = total + shift(block, "wt", -j, self.group).astype(F32)
        return total


def layer_forward(source, layout, params, early=None, fillers=(), last=False):
    gain_first, gain_second, w_proj, w_out, w_gate, w_up, w_down = params
    query_width = w_out.shape[0]
    head_size = (w_proj.shape[1] - query_width) // 2
    head_count = query_width // head_size
    width_all = source.shape[1] * layout.n_wt
    rows = layout.rows
    square = jnp.sum(source * source, axis=1)
    scaled = (source * gain_first).astype(BF)
    partial = jnp.concatenate([mm(scaled, w_proj).astype(BF), side_columns([square])], axis=1)
    total = reduce_rows(partial, "wt", fillers)
    proj_width = query_width + 2 * head_size
    square_all = total[:, proj_width] + total[:, proj_width + 1]
    inv_first = lax.rsqrt(square_all / width_all + EPS)
    projected = total[:, :proj_width] * inv_first[:, None]
    cosine, sine = rope(layout.query_pos, head_size)
    queries = rotate(
        projected[:, :query_width].reshape(rows, head_count, head_size), cosine[:, None], sine[:, None]
    ).astype(BF)
    key_rows = rotate(projected[:, query_width : query_width + head_size], cosine, sine).astype(BF)
    value_rows = projected[:, query_width + head_size :].astype(BF)
    pairs_all = layout.gather_keys(jnp.concatenate([key_rows, value_rows], axis=1))
    all_keys = pairs_all[:, :head_size]
    all_values = pairs_all[:, head_size:]
    query_rows = queries.reshape(rows * head_count, head_size)
    row_pos = jnp.repeat(layout.query_pos, head_count)
    raw = mm_nt(query_rows, all_keys) * head_size ** (-0.5)
    scores = jnp.where(layout.key_pos[None, :] <= row_pos[:, None], raw, NEG_FILL)
    row_max = jnp.max(scores, axis=1, keepdims=True)
    raised = jnp.exp(scores - row_max)
    log_total = row_max + jnp.log(jnp.sum(raised, axis=1, keepdims=True))
    probs = jnp.exp(scores - log_total)
    probs_low = probs.astype(BF)
    attended = mm(probs_low, all_values).astype(BF).reshape(rows, query_width)
    attended_full = gather_rows(attended, "wt")
    middle = source + mm(attended_full, w_out)
    middle_full = gather_cols(middle.astype(BF), "wt")
    if early is not None:
        middle_full, early = lax.optimization_barrier((middle_full, early))
        early = [early] + [shift(early, "wt", s) for s in range(1, layout.n_wt)]
    middle_full = middle_full.astype(F32)
    inv_second = lax.rsqrt(jnp.sum(middle_full * middle_full, axis=1) / width_all + EPS)
    normed_second = (middle_full * inv_second[:, None] * gain_second).astype(BF)
    gate_pre = mm(normed_second, w_gate)
    up_pre = mm(normed_second, w_up)
    hidden_act = (gelu_tanh(gate_pre) * up_pre).astype(BF)
    if early is not None:
        hidden_act, *early = lax.optimization_barrier((hidden_act, *early))
        early = join_cols(early, "wt")
    update = mm(hidden_act, w_down).astype(BF)
    saved = (
        source,
        inv_first,
        projected,
        query_rows,
        all_keys,
        all_values,
        probs,
        attended_full,
        middle,
        inv_second,
        normed_second,
        gate_pre,
        up_pre,
        hidden_act,
        cosine,
        sine,
    )
    if last:
        return update, saved, early
    return middle + reduce_cols(update, "wt"), saved, early


def layer_backward(grad_out, grad_full, layout, saved, params, behind=None):
    gain_first, gain_second, w_proj, w_out, w_gate, w_up, w_down = params
    (
        source,
        inv_first,
        projected,
        query_rows,
        all_keys,
        all_values,
        probs,
        attended_full,
        middle,
        inv_second,
        normed_second,
        gate_pre,
        up_pre,
        hidden_act,
        cosine,
        sine,
    ) = saved
    section_id = lax.axis_index("section")
    n_ctx = layout.n_ctx
    query_width = w_out.shape[0]
    proj_width = w_proj.shape[1]
    head_size = (proj_width - query_width) // 2
    head_count = query_width // head_size
    width_all = source.shape[1] * layout.n_wt
    rows = layout.rows
    score_scale = head_size ** (-0.5)
    attention_kept = None
    if behind is not None:
        attention_grads, sums = behind
        attention_grads = attention_grads()
        attention_kept = keep(*attention_grads)
        grad_full = gather_cols(grad_out.astype(BF), "wt", attention_grads + [sums])
    down = weight_grad(
        both_halves(section_id, *row_halves(grad_full, n_ctx)), both_sections(hidden_act)
    )
    down_kept = keep(down)
    if behind is None:
        (grad_full,) = after([grad_full], [down])
    d_hidden = mm_nt(grad_full, w_down)
    activated, pull_back = jax.vjp(gelu_tanh, gate_pre)
    d_gate = pull_back(d_hidden * up_pre)[0].astype(BF)
    d_up = (d_hidden * activated).astype(BF)
    inner_part = jnp.sum(d_gate.astype(F32) * gate_pre + d_up.astype(F32) * up_pre, axis=1)
    inner = sum_small(inner_part, "wt") / (inv_second * width_all)
    gate_up = weight_grad(both_sections(normed_second), both_halves(section_id, d_gate, d_up))
    gate_up_kept = keep(gate_up)
    d_normed = reduce_cols(
        (mm_nt(d_gate, w_gate) + mm_nt(d_up, w_up)).astype(BF), "wt", [gate_up] if behind is None else [down, gate_up]
    )
    gain_local = lax.dynamic_slice_in_dim(gain_second, lax.axis_index("wt") * source.shape[1], source.shape[1], 0)
    d_middle = (
        grad_out
        + inv_second[:, None] * d_normed * gain_local
        - middle * (inv_second**3 * inner)[:, None]
    )
    d_gain_second = jnp.sum(d_normed * middle * inv_second[:, None], axis=0)
    d_middle_low = d_middle.astype(BF)
    out_grad = weight_grad(
        both_halves(section_id, *row_halves(attended_full, n_ctx)), both_sections(d_middle_low)
    )
    waits = [down_kept if behind is None else attention_kept]
    d_attended = reduce_rows(mm_nt(d_middle_low, w_out).astype(BF), "wt", [out_grad] + waits).astype(BF)
    d_rows = d_attended.reshape(rows * head_count, head_size)
    probs_low = probs.astype(BF)
    d_values_all = mm_tn(probs_low, d_rows)
    d_probs = mm_nt(d_rows, all_values)
    delta = jnp.sum(probs * d_probs, axis=1, keepdims=True)
    d_scores = (probs * (d_probs - delta) * score_scale).astype(BF)
    d_query_rows = mm(d_scores, all_keys)
    d_keys_all = mm_tn(d_scores, query_rows)
    d_pairs = layout.reduce_keys(jnp.concatenate([d_keys_all, d_values_all], axis=1))
    d_query = rotate(
        d_query_rows.reshape(rows, head_count, head_size), cosine[:, None], -sine[:, None]
    ).reshape(rows, query_width)
    d_key = rotate(d_pairs[:, :head_size], cosine, -sine)
    d_projected = jnp.concatenate([d_query, d_key, d_pairs[:, head_size:]], axis=1).astype(BF)
    inner_own = jnp.sum(d_projected.astype(F32) * projected, axis=1) * inv_first * inv_first / width_all
    packed = gather_rows(jnp.concatenate([d_projected, side_columns([inv_first, inner_own])], axis=1), "wt")
    d_projected_full = packed[:, :proj_width]
    side = packed[:, proj_width : proj_width + 4].astype(F32)
    inv_full = side[:, 0:1] + side[:, 1:2]
    inner_full = side[:, 2:3] + side[:, 3:4]
    d_first = mm_nt(d_projected_full, w_proj)
    d_source = d_middle + inv_full * d_first * gain_first - source * inner_full
    d_gain_first = jnp.sum(d_first * source * inv_full, axis=0)
    normed_first = (source * inv_full * gain_first).astype(BF)

    def attention_grads():
        owned = by_owner(d_projected_full, query_width, head_size, n_ctx)
        proj_grad = weight_grad(
            both_halves(section_id, *row_halves(owned, n_ctx)), both_sections(normed_first)
        )
        return [out_grad, proj_grad]

    return d_source, (down_kept, gate_up_kept), attention_grads, attention_kept, d_gain_first, d_gain_second


def both_sections(value):
    return jnp.concatenate([value, shift(value, "section", 1)], axis=0)


def both_halves(section_id, low, high):
    own = jnp.where(section_id == 0, low, high)
    other = jnp.where(section_id == 0, high, low)
    return jnp.concatenate([own, shift(other, "section", 1)], axis=0)


def row_halves(value, n_ctx):
    part = value.shape[1] // n_ctx
    half = part // 2
    return tuple(
        jnp.concatenate([value[:, c * part + h * half : c * part + (h + 1) * half] for c in range(n_ctx)], axis=1)
        for h in range(2)
    )


def by_owner(value, query_width, head_size, n_ctx):
    query_part = query_width // n_ctx
    head_part = head_size // n_ctx
    pieces = []
    for c in range(n_ctx):
        pieces.append(value[:, c * query_part : (c + 1) * query_part])
        for base in (query_width, query_width + head_size):
            pieces.append(value[:, base + c * head_part : base + (c + 1) * head_part])
    return jnp.concatenate(pieces, axis=1)


def weight_grad(left, right):
    return natural(mm_tn(left, right).astype(BF))


def keep(*partials):
    n_ctx = lax.axis_size("ctx")
    joined = partials[0]
    if len(partials) > 1:
        blocks = [partial.reshape(n_ctx, -1, partial.shape[1]) for partial in partials]
        joined = jnp.concatenate(blocks, axis=1).reshape(-1, joined.shape[1])
    return lax.psum_scatter(joined, "ctx", scatter_dimension=0, tiled=True)


def home(section_id, first_block, second_block):
    kept = jnp.where(section_id == 0, first_block, second_block)
    sent = jnp.where(section_id == 0, second_block, first_block)
    received = shift(sent, "section", 1)
    low = jnp.where(section_id == 0, kept, received)
    high = jnp.where(section_id == 0, received, kept)
    return low, high


def local(hidden_in, out_grad, block_pos, norm1_gain, norm2_gain, wq, wk, wv, wo, w_gate, w_up, w_down):
    n_section = lax.axis_size("section")
    assert n_section == 2
    n_ctx = lax.axis_size("ctx")
    section_id = lax.axis_index("section")
    micro_count, row_count, width = hidden_in.shape
    micro_own = micro_count // n_section
    query_width = wq.shape[2]
    head_size = wk.shape[2]

    def fetch(weight):
        return lax.all_gather(weight, "section", axis=0, tiled=False)

    def fetch_fast(weight):
        received = shift(weight, "section", 1)
        return lax.optimization_barrier(
            (jnp.where(section_id == 0, weight, received), jnp.where(section_id == 0, received, weight))
        )

    w_proj = fetch_fast(jnp.concatenate([wq[0], wk[0], wv[0]], axis=1))
    weights = (w_proj, fetch(wo[0]), fetch(w_gate[0]), fetch(w_up[0]), fetch_fast(w_down[0]))
    gains = jnp.concatenate([norm1_gain, norm2_gain], axis=0)
    other_gains = shift(gains, "section", 1)
    gains = jnp.concatenate(
        [jnp.where(section_id == 0, gains, other_gains), jnp.where(section_id == 0, other_gains, gains)], axis=0
    )
    gains_full = gather_cols(gains, "wt")
    params = [
        (gains[2 * l], gains_full[2 * l + 1]) + tuple(w[l] for w in weights) for l in range(n_section)
    ]
    first_micro = section_id * micro_own
    layout = Layout(block_pos, first_micro, micro_own, row_count)

    def own_rows(value):
        return lax.dynamic_slice_in_dim(value, first_micro, micro_own, 0).reshape(micro_own * row_count, width)

    cotangent = own_rows(out_grad)
    state, saved_0, grad_full = layer_forward(
        own_rows(hidden_in).astype(F32), layout, params[0], cotangent, [params[0][6]]
    )
    update, saved_1, _ = layer_forward(state, layout, params[1], last=True)
    grad, feed_1, pending, _, d_first_1, d_second_1 = layer_backward(
        cotangent.astype(F32), grad_full, layout, saved_1, params[1]
    )
    in_grad_own, feed_0, pending, attention_1, d_first_0, d_second_0 = layer_backward(
        grad, None, layout, saved_0, params[0], (pending, feed_1[1])
    )
    attention_grads = pending()
    (update,) = after([update], attention_grads)
    out_own = (saved_1[8] + reduce_cols(update, "wt")).astype(BF)
    attention_0 = keep(*after(attention_grads, feed_0))

    def everywhere(own):
        low, high = own, shift(own, "section", 1)
        both = jnp.concatenate(
            [jnp.where(section_id == 0, low, high), jnp.where(section_id == 0, high, low)], axis=0
        )
        return both.reshape(micro_count, row_count, width)

    out = everywhere(out_own)
    in_grad = everywhere(in_grad_own)
    gain_sum = lax.psum(
        jnp.stack([jnp.stack([d_first_0, d_second_0]), jnp.stack([d_first_1, d_second_1])]), ("section", "ctx")
    )
    gain_mine = jnp.where(section_id == 0, gain_sum[0], gain_sum[1])
    down, gate_up = (home(section_id, a, b) for a, b in zip(feed_0, feed_1))
    grad_down = jnp.concatenate(down, axis=0).T.astype(F32)
    grad_gate, grad_up = (half.astype(F32) for half in gate_up)
    (attention_0,) = after([attention_0], [grad_down, grad_gate, grad_up, out, in_grad, gain_mine])
    low, high = home(section_id, attention_0, attention_1)
    out_rows = query_width // n_ctx // 2
    grad_wo = jnp.concatenate([low[:out_rows], high[:out_rows]], axis=0).astype(F32)
    grad_proj = jnp.concatenate([low[out_rows:], high[out_rows:]], axis=0).T.astype(F32)
    query_part = query_width // n_ctx
    head_part = head_size // n_ctx
    return (
        out,
        in_grad,
        grad_proj[:, :query_part][None],
        grad_proj[:, query_part : query_part + head_part][None],
        grad_proj[:, query_part + head_part :][None],
        grad_wo[None],
        grad_gate[None],
        grad_up[None],
        grad_down[None],
        gain_mine[0][None],
        gain_mine[1][None],
    )


def solution(mesh):
    return jax.shard_map(
        local,
        mesh=mesh,
        in_specs=(
            P(None, "ctx", "wt"),
            P(None, "ctx", "wt"),
            P(),
            P("section", "wt"),
            P("section", "wt"),
            P("section", "wt", None),
            P("section", "wt", None),
            P("section", "wt", None),
            P("section", None, "wt"),
            P("section", None, "wt"),
            P("section", None, "wt"),
            P("section", "wt", None),
        ),
        out_specs=(
            P(None, "ctx", "wt"),
            P(None, "ctx", "wt"),
            P("section", "wt", "ctx"),
            P("section", "wt", "ctx"),
            P("section", "wt", "ctx"),
            P("section", "ctx", "wt"),
            P("section", "ctx", "wt"),
            P("section", "ctx", "wt"),
            P("section", "wt", "ctx"),
            P("section", "wt"),
            P("section", "wt"),
        ),
        check_vma=False,
    )
```

```python
import math

import jax
import jax.numpy as jnp
from jax import lax
from jax.experimental.layout import Layout as ArrayLayout, with_layout_constraint
from jax.sharding import PartitionSpec as P

EPS = 1e-06
ROPE_LOG = math.log(10000.0)
NEG_FILL = -1e30
LANES = 128
BF = jnp.bfloat16
F32 = jnp.float32


def shift(value, axis, steps, group=None):
    count = lax.axis_size(axis)
    group = count if group is None else group
    pairs = [(i, i // group * group + (i % group + steps) % group) for i in range(count)]
    return lax.ppermute(value, axis, pairs)


def natural(value):
    return with_layout_constraint(value, ArrayLayout(major_to_minor=tuple(range(value.ndim))))


def after(values, fillers):
    if not fillers:
        return list(values)
    held = lax.optimization_barrier(tuple(values) + tuple(fillers))
    return list(held[: len(values)])


def mm(a, b):
    return jnp.dot(a, b, preferred_element_type=F32)


def mm_nt(a, b):
    return lax.dot_general(a, b, (((1,), (1,)), ((), ())), preferred_element_type=F32)


def mm_tn(a, b):
    return lax.dot_general(a, b, (((0,), (0,)), ((), ())), preferred_element_type=F32)


def pick(index, options):
    result = options[0]
    for number in range(1, len(options)):
        result = jnp.where(index == number, options[number], result)
    return result


def gather_cols(value, axis, fillers=()):
    count = lax.axis_size(axis)
    return join_cols([value] + after([shift(value, axis, s) for s in range(1, count)], fillers), axis)


def join_cols(parts, axis):
    me = lax.axis_index(axis)
    count = len(parts)
    return natural(jnp.concatenate([pick((me - place) % count, parts) for place in range(count)], axis=1))


def gather_rows(value, axis, fillers=()):
    count = lax.axis_size(axis)
    me = lax.axis_index(axis)
    rows = value.shape[0]
    full = jnp.zeros((count * rows, value.shape[1]), value.dtype)
    parts = [value] + after([shift(value, axis, s) for s in range(1, count)], fillers)
    for s in range(count):
        full = lax.dynamic_update_slice_in_dim(full, parts[s], (me - s) % count * rows, 0)
    return natural(full)


def reduce_rows(value, axis, fillers=()):
    count = lax.axis_size(axis)
    me = lax.axis_index(axis)
    rows = value.shape[0] // count
    blocks = [lax.dynamic_slice_in_dim(value, (me + s) % count * rows, rows, 0) for s in range(count)]
    received = after([shift(blocks[s], axis, s) for s in range(1, count)], fillers)
    return sum((part.astype(F32) for part in received), blocks[0].astype(F32))


def send_cols(value, axis):
    count = lax.axis_size(axis)
    me = lax.axis_index(axis)
    width = value.shape[1] // count
    blocks = [value[:, p * width : (p + 1) * width] for p in range(count)]
    chosen = [pick((me + s) % count, blocks) for s in range(count)]
    return [chosen[0]] + [shift(chosen[s], axis, s) for s in range(1, count)]


def add_up(parts):
    return sum((part.astype(F32) for part in parts[1:]), parts[0].astype(F32))


def reduce_cols(value, axis, fillers=()):
    own, *received = send_cols(value, axis)
    return add_up([own] + after(received, fillers))


def sum_small(value, axis):
    total = value
    for s in range(1, lax.axis_size(axis)):
        total = total + shift(value, axis, s)
    return total


def split_two(value):
    high = lax.reduce_precision(value, 8, 7)
    return high, value - high


def side_columns(terms):
    rows = terms[0].shape[0]
    column = lax.broadcasted_iota(jnp.int32, (rows, LANES), 1)
    block = jnp.zeros((rows, LANES), F32)
    for number, term in enumerate(terms):
        high, low = split_two(term)
        block = jnp.where(column == 2 * number, high[:, None], block)
        block = jnp.where(column == 2 * number + 1, low[:, None], block)
    return block.astype(BF)


def rope(positions, head_size):
    half = head_size // 2
    freqs = jnp.exp(jnp.arange(half, dtype=F32) * (-2.0 * ROPE_LOG / head_size))
    angles = positions.astype(F32)[:, None] * freqs
    return jnp.cos(angles), jnp.sin(angles)


def rotate(values, cosine, sine):
    half = values.shape[-1] // 2
    first = values[..., :half]
    second = values[..., half:]
    return jnp.concatenate([first * cosine - second * sine, second * cosine + first * sine], axis=-1)


def gelu_tanh(values):
    return jax.nn.gelu(values, approximate=True)


class Layout:
    def __init__(self, block_pos, first_micro, micros, row_count):
        self.n_wt = lax.axis_size("wt")
        self.n_ctx = lax.axis_size("ctx")
        self.group = self.n_wt // micros
        wt = lax.axis_index("wt")
        ctx = lax.axis_index("ctx")
        self.rows = row_count // self.group
        block_row = lax.dynamic_index_in_dim(block_pos, first_micro + wt // self.group, 0, keepdims=False)
        block_len = row_count * self.n_ctx // block_pos.shape[1]
        mine = wt % self.group

        def positions(ctx_at, group_at):
            places = ctx_at * row_count + group_at * self.rows + jnp.arange(self.rows, dtype=jnp.int32)
            blocks = (places // block_len)[:, None] == jnp.arange(block_row.shape[0], dtype=jnp.int32)[None, :]
            return jnp.sum(jnp.where(blocks, block_row[None, :], 0), axis=1) * block_len + places % block_len

        self.query_pos = positions(ctx, mine)
        self.key_pos = jnp.concatenate(
            [
                positions((ctx - s) % self.n_ctx, (mine - j) % self.group)
                for s in range(self.n_ctx)
                for j in range(self.group)
            ]
        )

    def gather_keys(self, rows):
        near = jnp.concatenate([rows] + [shift(rows, "wt", j, self.group) for j in range(1, self.group)], axis=0)
        return jnp.concatenate([near] + [shift(near, "ctx", s) for s in range(1, self.n_ctx)], axis=0)

    def reduce_keys(self, rows):
        near_rows = self.rows * self.group
        near = rows[:near_rows].astype(F32)
        for s in range(1, self.n_ctx):
            near = near + shift(rows[s * near_rows : (s + 1) * near_rows].astype(BF), "ctx", -s).astype(F32)
        total = near[: self.rows]
        for j in range(1, self.group):
            block = near[j * self.rows : (j + 1) * self.rows].astype(BF)
            total = total + shift(block, "wt", -j, self.group).astype(F32)
        return total


def layer_forward(source, layout, params, early=None, fillers=(), last=False):
    gain_first, gain_second, w_proj, w_out, w_gate, w_up, w_down = params
    query_width = w_out.shape[0]
    head_size = (w_proj.shape[1] - query_width) // 2
    head_count = query_width // head_size
    width_all = source.shape[1] * layout.n_wt
    rows = layout.rows
    square = jnp.sum(source * source, axis=1)
    scaled = (source * gain_first).astype(BF)
    partial = jnp.concatenate([mm(scaled, w_proj).astype(BF), side_columns([square])], axis=1)
    if callable(gain_second):
        partial, gain_second = gain_second(partial)
    total = reduce_rows(partial, "wt", fillers)
    proj_width = query_width + 2 * head_size
    square_all = total[:, proj_width] + total[:, proj_width + 1]
    inv_first = lax.rsqrt(square_all / width_all + EPS)
    projected = total[:, :proj_width] * inv_first[:, None]
    cosine, sine = rope(layout.query_pos, head_size)
    queries = rotate(
        projected[:, :query_width].reshape(rows, head_count, head_size), cosine[:, None], sine[:, None]
    ).astype(BF)
    key_rows = rotate(projected[:, query_width : query_width + head_size], cosine, sine).astype(BF)
    value_rows = projected[:, query_width + head_size :].astype(BF)
    pairs_all = layout.gather_keys(jnp.concatenate([key_rows, value_rows], axis=1))
    all_keys = pairs_all[:, :head_size]
    all_values = pairs_all[:, head_size:]
    query_rows = queries.reshape(rows * head_count, head_size)
    row_pos = jnp.repeat(layout.query_pos, head_count)
    raw = mm_nt(query_rows, all_keys) * head_size ** (-0.5)
    scores = jnp.where(layout.key_pos[None, :] <= row_pos[:, None], raw, NEG_FILL)
    row_max = jnp.max(scores, axis=1, keepdims=True)
    raised = jnp.exp(scores - row_max)
    log_total = row_max + jnp.log(jnp.sum(raised, axis=1, keepdims=True))
    probs = jnp.exp(scores - log_total)
    probs_low = probs.astype(BF)
    attended = mm(probs_low, all_values).astype(BF).reshape(rows, query_width)
    attended_full = gather_rows(attended, "wt")
    middle = source + mm(attended_full, w_out)
    middle_full = gather_cols(middle.astype(BF), "wt")
    if early is not None:
        middle_full, early = lax.optimization_barrier((middle_full, early))
        early = [early] + [shift(early, "wt", s) for s in range(1, layout.n_wt)]
    middle_full = middle_full.astype(F32)
    inv_second = lax.rsqrt(jnp.sum(middle_full * middle_full, axis=1) / width_all + EPS)
    normed_second = (middle_full * inv_second[:, None] * gain_second).astype(BF)
    gate_pre = mm(normed_second, w_gate)
    up_pre = mm(normed_second, w_up)
    hidden_act = (gelu_tanh(gate_pre) * up_pre).astype(BF)
    if early is not None:
        hidden_act, *early = lax.optimization_barrier((hidden_act, *early))
        early = join_cols(early, "wt")
    update = mm(hidden_act, w_down).astype(BF)
    saved = (
        source,
        inv_first,
        projected,
        query_rows,
        all_keys,
        all_values,
        probs,
        attended_full,
        middle,
        inv_second,
        normed_second,
        gate_pre,
        up_pre,
        hidden_act,
        cosine,
        sine,
    )
    if last:
        return update, saved, early
    return middle + reduce_cols(update, "wt"), saved, early


def layer_backward(grad_out, grad_full, layout, saved, params, behind=None):
    gain_first, gain_second, w_proj, w_out, w_gate, w_up, w_down = params
    (
        source,
        inv_first,
        projected,
        query_rows,
        all_keys,
        all_values,
        probs,
        attended_full,
        middle,
        inv_second,
        normed_second,
        gate_pre,
        up_pre,
        hidden_act,
        cosine,
        sine,
    ) = saved
    section_id = lax.axis_index("section")
    n_ctx = layout.n_ctx
    query_width = w_out.shape[0]
    proj_width = w_proj.shape[1]
    head_size = (proj_width - query_width) // 2
    head_count = query_width // head_size
    width_all = source.shape[1] * layout.n_wt
    rows = layout.rows
    score_scale = head_size ** (-0.5)
    attention_kept = None
    output_parts = None
    if behind is not None:
        attention_grads, sums, update = behind
        attention_grads = attention_grads()
        attention_kept = keep_fast(attention_grads)
        grad_full = gather_cols(grad_out.astype(BF), "wt", attention_grads + [sums])
        output_parts = send_cols(*after([update], [grad_full]), "wt")
    down = weight_grad(
        both_halves(section_id, *row_halves(grad_full, n_ctx)), both_sections(hidden_act)
    )
    down_kept = keep(down)
    if behind is None:
        (grad_full,) = after([grad_full], [down])
    d_hidden = mm_nt(grad_full, w_down)
    activated, pull_back = jax.vjp(gelu_tanh, gate_pre)
    d_gate = pull_back(d_hidden * up_pre)[0].astype(BF)
    d_up = (d_hidden * activated).astype(BF)
    inner_part = jnp.sum(d_gate.astype(F32) * gate_pre + d_up.astype(F32) * up_pre, axis=1)
    d_normed_part = (mm_nt(d_gate, w_gate) + mm_nt(d_up, w_up)).astype(BF)
    if output_parts is not None:
        d_normed_part, *output_parts = lax.optimization_barrier((d_normed_part, *output_parts))
    inner_part, normed_other = after([inner_part, shift(normed_second, "section", 1)], [d_normed_part])
    inner = sum_small(inner_part, "wt") / (inv_second * width_all)
    gate_up = weight_grad(
        jnp.concatenate([normed_second, normed_other], axis=0), both_halves(section_id, d_gate, d_up)
    )
    gate_up_kept = keep(gate_up)
    d_normed = reduce_cols(d_normed_part, "wt", [gate_up] if behind is None else [down, gate_up])
    gain_local = lax.dynamic_slice_in_dim(gain_second, lax.axis_index("wt") * source.shape[1], source.shape[1], 0)
    d_middle = (
        grad_out
        + inv_second[:, None] * d_normed * gain_local
        - middle * (inv_second**3 * inner)[:, None]
    )
    d_gain_second = jnp.sum(d_normed * middle * inv_second[:, None], axis=0)
    d_middle_low = d_middle.astype(BF)
    out_grad = weight_grad(
        both_halves(section_id, *row_halves(attended_full, n_ctx)), both_sections(d_middle_low)
    )
    waits = [down_kept if behind is None else attention_kept]
    d_attended = reduce_rows(mm_nt(d_middle_low, w_out).astype(BF), "wt", [out_grad] + waits).astype(BF)
    d_rows = d_attended.reshape(rows * head_count, head_size)
    probs_low = probs.astype(BF)
    d_values_all = mm_tn(probs_low, d_rows)
    d_probs = mm_nt(d_rows, all_values)
    delta = jnp.sum(probs * d_probs, axis=1, keepdims=True)
    d_scores = (probs * (d_probs - delta) * score_scale).astype(BF)
    d_query_rows = mm(d_scores, all_keys)
    d_keys_all = mm_tn(d_scores, query_rows)
    d_query = rotate(
        d_query_rows.reshape(rows, head_count, head_size), cosine[:, None], -sine[:, None]
    ).reshape(rows, query_width).astype(BF)
    d_query_full = gather_rows(d_query, "wt")
    d_pairs = layout.reduce_keys(jnp.concatenate([d_keys_all, d_values_all], axis=1))
    d_key = rotate(d_pairs[:, :head_size], cosine, -sine)
    d_pairs = jnp.concatenate([d_key, d_pairs[:, head_size:]], axis=1).astype(BF)
    inner_own = jnp.sum(d_query.astype(F32) * projected[:, :query_width], axis=1)
    inner_own = inner_own + jnp.sum(d_pairs.astype(F32) * projected[:, query_width:], axis=1)
    inner_own = inner_own * inv_first * inv_first / width_all
    packed = gather_rows(jnp.concatenate([d_pairs, side_columns([inv_first, inner_own])], axis=1), "wt")
    d_projected_full = natural(jnp.concatenate([d_query_full, packed[:, : 2 * head_size]], axis=1))
    side = packed[:, 2 * head_size : 2 * head_size + 4].astype(F32)
    inv_full = side[:, 0:1] + side[:, 1:2]
    inner_full = side[:, 2:3] + side[:, 3:4]
    d_first = mm_nt(d_projected_full, w_proj)
    d_source = d_middle + inv_full * d_first * gain_first - source * inner_full
    d_gain_first = jnp.sum(d_first * source * inv_full, axis=0)
    normed_first = (source * inv_full * gain_first).astype(BF)

    def attention_grads():
        owned = by_owner(d_projected_full, query_width, head_size, n_ctx)
        proj_grad = weight_grad(
            both_halves(section_id, *row_halves(owned, n_ctx)), both_sections(normed_first)
        )
        return [out_grad, proj_grad]

    output = None if output_parts is None else add_up(output_parts)
    return d_source, (down_kept, gate_up_kept), attention_grads, attention_kept, d_gain_first, d_gain_second, output


def both_sections(value):
    return jnp.concatenate([value, shift(value, "section", 1)], axis=0)


def both_halves(section_id, low, high):
    own = jnp.where(section_id == 0, low, high)
    other = jnp.where(section_id == 0, high, low)
    return jnp.concatenate([own, shift(other, "section", 1)], axis=0)


def row_halves(value, n_ctx):
    part = value.shape[1] // n_ctx
    half = part // 2
    return tuple(
        jnp.concatenate([value[:, c * part + h * half : c * part + (h + 1) * half] for c in range(n_ctx)], axis=1)
        for h in range(2)
    )


def by_owner(value, query_width, head_size, n_ctx):
    query_part = query_width // n_ctx
    head_part = head_size // n_ctx
    pieces = []
    for c in range(n_ctx):
        pieces.append(value[:, c * query_part : (c + 1) * query_part])
        for base in (query_width, query_width + head_size):
            pieces.append(value[:, base + c * head_part : base + (c + 1) * head_part])
    return jnp.concatenate(pieces, axis=1)


def weight_grad(left, right):
    return natural(mm_tn(left, right).astype(BF))


def keep(partial):
    return lax.psum_scatter(partial, "ctx", scatter_dimension=0, tiled=True)


def keep_fast(partials):
    n_ctx = lax.axis_size("ctx")
    blocks = [partial.reshape(n_ctx, -1, partial.shape[1]) for partial in partials]
    joined = jnp.concatenate(blocks, axis=1)
    return reduce_rows(joined.reshape(-1, joined.shape[2]), "ctx").astype(BF)


def home(section_id, first_block, second_block):
    kept = jnp.where(section_id == 0, first_block, second_block)
    sent = jnp.where(section_id == 0, second_block, first_block)
    received = shift(sent, "section", 1)
    low = jnp.where(section_id == 0, kept, received)
    high = jnp.where(section_id == 0, received, kept)
    return low, high


def local(hidden_in, out_grad, block_pos, norm1_gain, norm2_gain, wq, wk, wv, wo, w_gate, w_up, w_down):
    n_section = lax.axis_size("section")
    assert n_section == 2
    n_ctx = lax.axis_size("ctx")
    section_id = lax.axis_index("section")
    micro_count, row_count, width = hidden_in.shape
    micro_own = micro_count // n_section
    query_width = wq.shape[2]
    head_size = wk.shape[2]

    def fetch(weight):
        return lax.all_gather(weight, "section", axis=0, tiled=False)

    def fetch_fast(weight):
        received = shift(weight, "section", 1)
        return lax.optimization_barrier(
            (jnp.where(section_id == 0, weight, received), jnp.where(section_id == 0, received, weight))
        )

    gains = jnp.concatenate([norm1_gain, norm2_gain], axis=0)
    other_gains = shift(gains, "section", 1)
    other_proj = jnp.concatenate(
        [shift(wq[0], "section", 1), shift(jnp.concatenate([wk[0], wv[0]], axis=1), "section", 1)], axis=1
    )
    own_proj = jnp.concatenate([wq[0], wk[0], wv[0]], axis=1)
    w_proj = lax.optimization_barrier(
        (jnp.where(section_id == 0, own_proj, other_proj), jnp.where(section_id == 0, other_proj, own_proj))
    )
    weights = (w_proj, fetch(wo[0]), fetch(w_gate[0]), fetch(w_up[0]), fetch_fast(after([w_down[0]], [other_proj])[0]))
    gains = [jnp.where(section_id == 0, gains, other_gains), jnp.where(section_id == 0, other_gains, gains)]
    second_full = []

    def gather_second(partial):
        own, partial = lax.optimization_barrier((jnp.stack([gains[0][1], gains[1][1]]), partial))
        second_full.append(gather_cols(own, "wt"))
        return partial, second_full[0][0]

    params = [[gains[l][0], gather_second] + [w[l] for w in weights] for l in range(n_section)]
    first_micro = section_id * micro_own
    layout = Layout(block_pos, first_micro, micro_own, row_count)

    def own_rows(value):
        return lax.dynamic_slice_in_dim(value, first_micro, micro_own, 0).reshape(micro_own * row_count, width)

    cotangent = own_rows(out_grad)
    state, saved_0, grad_full = layer_forward(
        own_rows(hidden_in).astype(F32), layout, params[0], cotangent, [params[0][6]]
    )
    for l in range(n_section):
        params[l][1] = second_full[0][l]
    update, saved_1, _ = layer_forward(state, layout, params[1], last=True)
    grad, feed_1, pending, _, d_first_1, d_second_1, _ = layer_backward(
        cotangent.astype(F32), grad_full, layout, saved_1, params[1]
    )
    in_grad_own, feed_0, pending, attention_1, d_first_0, d_second_0, update = layer_backward(
        grad, None, layout, saved_0, params[0], (pending, feed_1[1], update)
    )
    out_own = (saved_1[8] + update).astype(BF)
    attention_0 = keep_fast(pending())

    def everywhere(own):
        low, high = own, shift(own, "section", 1)
        both = jnp.concatenate(
            [jnp.where(section_id == 0, low, high), jnp.where(section_id == 0, high, low)], axis=0
        )
        return both.reshape(micro_count, row_count, width)

    out = everywhere(out_own)
    in_grad = everywhere(in_grad_own)
    gain_sum = lax.psum(
        jnp.stack([jnp.stack([d_first_0, d_second_0]), jnp.stack([d_first_1, d_second_1])]), ("section", "ctx")
    )
    gain_mine = jnp.where(section_id == 0, gain_sum[0], gain_sum[1])
    down, gate_up = (home(section_id, a, b) for a, b in zip(feed_0, feed_1))
    grad_down = jnp.concatenate(down, axis=0).T.astype(F32)
    grad_gate, grad_up = (half.astype(F32) for half in gate_up)
    (attention_0,) = after([attention_0], [grad_down, grad_gate, grad_up, out, in_grad, gain_mine])
    low, high = home(section_id, attention_0, attention_1)
    out_rows = query_width // n_ctx // 2
    grad_wo = jnp.concatenate([low[:out_rows], high[:out_rows]], axis=0).astype(F32)
    grad_proj = jnp.concatenate([low[out_rows:], high[out_rows:]], axis=0).T.astype(F32)
    query_part = query_width // n_ctx
    head_part = head_size // n_ctx
    return (
        out,
        in_grad,
        grad_proj[:, :query_part][None],
        grad_proj[:, query_part : query_part + head_part][None],
        grad_proj[:, query_part + head_part :][None],
        grad_wo[None],
        grad_gate[None],
        grad_up[None],
        grad_down[None],
        gain_mine[0][None],
        gain_mine[1][None],
    )


def solution(mesh):
    return jax.shard_map(
        local,
        mesh=mesh,
        in_specs=(
            P(None, "ctx", "wt"),
            P(None, "ctx", "wt"),
            P(),
            P("section", "wt"),
            P("section", "wt"),
            P("section", "wt", None),
            P("section", "wt", None),
            P("section", "wt", None),
            P("section", None, "wt"),
            P("section", None, "wt"),
            P("section", None, "wt"),
            P("section", "wt", None),
        ),
        out_specs=(
            P(None, "ctx", "wt"),
            P(None, "ctx", "wt"),
            P("section", "wt", "ctx"),
            P("section", "wt", "ctx"),
            P("section", "wt", "ctx"),
            P("section", "ctx", "wt"),
            P("section", "ctx", "wt"),
            P("section", "ctx", "wt"),
            P("section", "wt", "ctx"),
            P("section", "wt"),
            P("section", "wt"),
        ),
        check_vma=False,
    )
```

```python
import math

import jax
import jax.numpy as jnp
from jax import lax
from jax.experimental.layout import Layout as ArrayLayout, with_layout_constraint
from jax.sharding import PartitionSpec as P

EPS = 1e-06
ROPE_LOG = math.log(10000.0)
NEG_FILL = -1e30
LANES = 128
BF = jnp.bfloat16
F32 = jnp.float32


def shift(value, axis, steps, group=None):
    count = lax.axis_size(axis)
    group = count if group is None else group
    pairs = [(i, i // group * group + (i % group + steps) % group) for i in range(count)]
    return lax.ppermute(value, axis, pairs)


def natural(value):
    return with_layout_constraint(value, ArrayLayout(major_to_minor=tuple(range(value.ndim))))


def after(values, fillers):
    if not fillers:
        return list(values)
    held = lax.optimization_barrier(tuple(values) + tuple(fillers))
    return list(held[: len(values)])


def mm(a, b):
    return jnp.dot(a, b, preferred_element_type=F32)


def mm_nt(a, b):
    return lax.dot_general(a, b, (((1,), (1,)), ((), ())), preferred_element_type=F32)


def mm_tn(a, b):
    return lax.dot_general(a, b, (((0,), (0,)), ((), ())), preferred_element_type=F32)


def pick(index, options):
    result = options[0]
    for number in range(1, len(options)):
        result = jnp.where(index == number, options[number], result)
    return result


def gather_cols(value, axis, fillers=()):
    count = lax.axis_size(axis)
    return join_cols([value] + after([shift(value, axis, s) for s in range(1, count)], fillers), axis)


def join_cols(parts, axis):
    me = lax.axis_index(axis)
    count = len(parts)
    return natural(jnp.concatenate([pick((me - place) % count, parts) for place in range(count)], axis=1))


def gather_rows(value, axis, fillers=()):
    count = lax.axis_size(axis)
    me = lax.axis_index(axis)
    rows = value.shape[0]
    full = jnp.zeros((count * rows, value.shape[1]), value.dtype)
    parts = [value] + after([shift(value, axis, s) for s in range(1, count)], fillers)
    for s in range(count):
        full = lax.dynamic_update_slice_in_dim(full, parts[s], (me - s) % count * rows, 0)
    return natural(full)


def reduce_rows(value, axis, fillers=()):
    own, *received = send_rows(value, axis)
    return add_up([own] + after(received, fillers))


def send_rows(value, axis):
    count = lax.axis_size(axis)
    me = lax.axis_index(axis)
    rows = value.shape[0] // count
    blocks = [lax.dynamic_slice_in_dim(value, (me + s) % count * rows, rows, 0) for s in range(count)]
    return [blocks[0]] + [shift(blocks[s], axis, s) for s in range(1, count)]


def send_cols(value, axis):
    count = lax.axis_size(axis)
    me = lax.axis_index(axis)
    width = value.shape[1] // count
    blocks = [value[:, p * width : (p + 1) * width] for p in range(count)]
    chosen = [pick((me + s) % count, blocks) for s in range(count)]
    return [chosen[0]] + [shift(chosen[s], axis, s) for s in range(1, count)]


def add_up(parts):
    return sum((part.astype(F32) for part in parts[1:]), parts[0].astype(F32))


def reduce_cols(value, axis, fillers=()):
    own, *received = send_cols(value, axis)
    return add_up([own] + after(received, fillers))


def sum_small(value, axis):
    total = value
    for s in range(1, lax.axis_size(axis)):
        total = total + shift(value, axis, s)
    return total


def sum_in_order(value, axis):
    count = lax.axis_size(axis)
    me = lax.axis_index(axis)
    parts = [value] + [shift(value, axis, s) for s in range(1, count)]
    return sum(pick((me - place) % count, parts) for place in range(count))


def split_two(value):
    high = lax.reduce_precision(value, 8, 7)
    return high, value - high


def side_columns(terms):
    rows = terms[0].shape[0]
    column = lax.broadcasted_iota(jnp.int32, (rows, LANES), 1)
    block = jnp.zeros((rows, LANES), F32)
    for number, term in enumerate(terms):
        high, low = split_two(term)
        block = jnp.where(column == 2 * number, high[:, None], block)
        block = jnp.where(column == 2 * number + 1, low[:, None], block)
    return block.astype(BF)


def rope(positions, head_size):
    half = head_size // 2
    freqs = jnp.exp(jnp.arange(half, dtype=F32) * (-2.0 * ROPE_LOG / head_size))
    angles = positions.astype(F32)[:, None] * freqs
    return jnp.cos(angles), jnp.sin(angles)


def rotate(values, cosine, sine):
    half = values.shape[-1] // 2
    first = values[..., :half]
    second = values[..., half:]
    return jnp.concatenate([first * cosine - second * sine, second * cosine + first * sine], axis=-1)


def gelu_tanh(values):
    return jax.nn.gelu(values, approximate=True)


class Layout:
    def __init__(self, block_pos, first_micro, micros, row_count):
        self.n_wt = lax.axis_size("wt")
        self.n_ctx = lax.axis_size("ctx")
        self.group = self.n_wt // micros
        wt = lax.axis_index("wt")
        ctx = lax.axis_index("ctx")
        self.rows = row_count // self.group
        block_row = lax.dynamic_index_in_dim(block_pos, first_micro + wt // self.group, 0, keepdims=False)
        block_len = row_count * self.n_ctx // block_pos.shape[1]
        mine = wt % self.group

        def positions(ctx_at, group_at):
            places = ctx_at * row_count + group_at * self.rows + jnp.arange(self.rows, dtype=jnp.int32)
            blocks = (places // block_len)[:, None] == jnp.arange(block_row.shape[0], dtype=jnp.int32)[None, :]
            return jnp.sum(jnp.where(blocks, block_row[None, :], 0), axis=1) * block_len + places % block_len

        self.query_pos = positions(ctx, mine)
        self.key_pos = jnp.concatenate(
            [
                positions((ctx - s) % self.n_ctx, (mine - j) % self.group)
                for s in range(self.n_ctx)
                for j in range(self.group)
            ]
        )

    def gather_keys(self, rows):
        near = jnp.concatenate([rows] + [shift(rows, "wt", j, self.group) for j in range(1, self.group)], axis=0)
        return jnp.concatenate([near] + [shift(near, "ctx", s) for s in range(1, self.n_ctx)], axis=0)

    def reduce_keys(self, rows):
        near_rows = self.rows * self.group
        near = rows[:near_rows].astype(F32)
        for s in range(1, self.n_ctx):
            near = near + shift(rows[s * near_rows : (s + 1) * near_rows].astype(BF), "ctx", -s).astype(F32)
        total = near[: self.rows]
        for j in range(1, self.group):
            block = near[j * self.rows : (j + 1) * self.rows].astype(BF)
            total = total + shift(block, "wt", -j, self.group).astype(F32)
        return total


def layer_forward(source, layout, params, early=None, fillers=(), last=False):
    gain_first, gain_second, w_proj, w_out, w_gate, w_up, w_down = params
    query_width = w_out.shape[0]
    head_size = (w_proj.shape[1] - query_width) // 2
    head_count = query_width // head_size
    width_all = source.shape[1] * layout.n_wt
    rows = layout.rows
    square = jnp.sum(source * source, axis=1)
    scaled = (source * gain_first).astype(BF)
    partial = jnp.concatenate([mm(scaled, w_proj).astype(BF), side_columns([square])], axis=1)
    total = reduce_rows(partial, "wt", fillers)
    if callable(gain_second):
        total, gain_second = gain_second(total)
    proj_width = query_width + 2 * head_size
    square_all = total[:, proj_width] + total[:, proj_width + 1]
    inv_first = lax.rsqrt(square_all / width_all + EPS)
    projected = total[:, :proj_width] * inv_first[:, None]
    cosine, sine = rope(layout.query_pos, head_size)
    queries = rotate(
        projected[:, :query_width].reshape(rows, head_count, head_size), cosine[:, None], sine[:, None]
    ).astype(BF)
    key_rows = rotate(projected[:, query_width : query_width + head_size], cosine, sine).astype(BF)
    value_rows = projected[:, query_width + head_size :].astype(BF)
    pairs_all = layout.gather_keys(jnp.concatenate([key_rows, value_rows], axis=1))
    all_keys = pairs_all[:, :head_size]
    all_values = pairs_all[:, head_size:]
    query_rows = queries.reshape(rows * head_count, head_size)
    row_pos = jnp.repeat(layout.query_pos, head_count)
    raw = mm_nt(query_rows, all_keys) * head_size ** (-0.5)
    scores = jnp.where(layout.key_pos[None, :] <= row_pos[:, None], raw, NEG_FILL)
    row_max = jnp.max(scores, axis=1, keepdims=True)
    raised = jnp.exp(scores - row_max)
    log_total = row_max + jnp.log(jnp.sum(raised, axis=1, keepdims=True))
    probs = jnp.exp(scores - log_total)
    probs_low = probs.astype(BF)
    attended = mm(probs_low, all_values).astype(BF).reshape(rows, query_width)
    attended_full = gather_rows(attended, "wt")
    middle = source + mm(attended_full, w_out)
    middle_full = gather_cols(middle.astype(BF), "wt")
    if early is not None:
        middle_full, early = lax.optimization_barrier((middle_full, early))
        early = [early] + [shift(early, "wt", s) for s in range(1, layout.n_wt)]
    middle_full = middle_full.astype(F32)
    inv_second = lax.rsqrt(jnp.sum(middle_full * middle_full, axis=1) / width_all + EPS)
    normed_second = (middle_full * inv_second[:, None] * gain_second).astype(BF)
    gate_pre = mm(normed_second, w_gate)
    up_pre = mm(normed_second, w_up)
    hidden_act = (gelu_tanh(gate_pre) * up_pre).astype(BF)
    if early is not None:
        hidden_act, *early = lax.optimization_barrier((hidden_act, *early))
        early = join_cols(early, "wt")
    update = mm(hidden_act, w_down).astype(BF)
    saved = (
        source,
        inv_first,
        projected,
        query_rows,
        all_keys,
        all_values,
        probs,
        attended_full,
        middle,
        inv_second,
        normed_second,
        gate_pre,
        up_pre,
        hidden_act,
        cosine,
        sine,
    )
    if last:
        return update, saved, early
    return middle + reduce_cols(update, "wt"), saved, early


def layer_backward(grad_out, grad_full, layout, saved, params, behind=None):
    gain_first, gain_second, w_proj, w_out, w_gate, w_up, w_down = params
    (
        source,
        inv_first,
        projected,
        query_rows,
        all_keys,
        all_values,
        probs,
        attended_full,
        middle,
        inv_second,
        normed_second,
        gate_pre,
        up_pre,
        hidden_act,
        cosine,
        sine,
    ) = saved
    section_id = lax.axis_index("section")
    n_ctx = layout.n_ctx
    query_width = w_out.shape[0]
    proj_width = w_proj.shape[1]
    head_size = (proj_width - query_width) // 2
    head_count = query_width // head_size
    width_all = source.shape[1] * layout.n_wt
    rows = layout.rows
    score_scale = head_size ** (-0.5)
    attention_kept = None
    if behind is not None:
        attention_grads, sums = behind
        attention_grads = attention_grads()
        attention_kept = keep(*attention_grads)
        grad_full = gather_cols(grad_out.astype(BF), "wt", attention_grads + [sums])
    down = weight_grad(
        both_halves(section_id, *row_halves(grad_full, n_ctx)), both_sections(hidden_act)
    )
    down_kept = keep(down)
    if behind is None:
        (grad_full,) = after([grad_full], [down])
    d_hidden = mm_nt(grad_full, w_down)
    activated, pull_back = jax.vjp(gelu_tanh, gate_pre)
    d_gate = pull_back(d_hidden * up_pre)[0].astype(BF)
    d_up = (d_hidden * activated).astype(BF)
    inner_part = jnp.sum(d_gate.astype(F32) * gate_pre + d_up.astype(F32) * up_pre, axis=1)
    d_normed_part = (mm_nt(d_gate, w_gate) + mm_nt(d_up, w_up)).astype(BF)
    inner_part, normed_other = after([inner_part, shift(normed_second, "section", 1)], [d_normed_part])
    inner = sum_small(inner_part, "wt") / (inv_second * width_all)
    gate_up = weight_grad(
        jnp.concatenate([normed_second, normed_other], axis=0), both_halves(section_id, d_gate, d_up)
    )
    gate_up_kept = keep(gate_up)
    d_normed = reduce_cols(d_normed_part, "wt", [gate_up] if behind is None else [down, gate_up])
    gain_local = lax.dynamic_slice_in_dim(gain_second, lax.axis_index("wt") * source.shape[1], source.shape[1], 0)
    d_middle = (
        grad_out
        + inv_second[:, None] * d_normed * gain_local
        - middle * (inv_second**3 * inner)[:, None]
    )
    d_gain_second = jnp.sum(d_normed * middle * inv_second[:, None], axis=0)
    d_middle_low = d_middle.astype(BF)
    out_grad = weight_grad(
        both_halves(section_id, *row_halves(attended_full, n_ctx)), both_sections(d_middle_low)
    )
    waits = [down_kept if behind is None else attention_kept]
    d_attended = reduce_rows(mm_nt(d_middle_low, w_out).astype(BF), "wt", [out_grad] + waits).astype(BF)
    d_rows = d_attended.reshape(rows * head_count, head_size)
    probs_low = probs.astype(BF)
    d_values_all = mm_tn(probs_low, d_rows)
    d_probs = mm_nt(d_rows, all_values)
    delta = jnp.sum(probs * d_probs, axis=1, keepdims=True)
    d_scores = (probs * (d_probs - delta) * score_scale).astype(BF)
    d_query_rows = mm(d_scores, all_keys)
    d_keys_all = mm_tn(d_scores, query_rows)
    d_query = rotate(
        d_query_rows.reshape(rows, head_count, head_size), cosine[:, None], -sine[:, None]
    ).reshape(rows, query_width).astype(BF)
    d_query_full = gather_rows(d_query, "wt")
    d_pairs = layout.reduce_keys(jnp.concatenate([d_keys_all, d_values_all], axis=1))
    d_key = rotate(d_pairs[:, :head_size], cosine, -sine)
    d_pairs = jnp.concatenate([d_key, d_pairs[:, head_size:]], axis=1).astype(BF)
    inner_own = jnp.sum(d_query.astype(F32) * projected[:, :query_width], axis=1)
    inner_own = inner_own + jnp.sum(d_pairs.astype(F32) * projected[:, query_width:], axis=1)
    inner_own = inner_own * inv_first * inv_first / width_all
    packed = gather_rows(jnp.concatenate([d_pairs, side_columns([inv_first, inner_own])], axis=1), "wt")
    d_projected_full = natural(jnp.concatenate([d_query_full, packed[:, : 2 * head_size]], axis=1))
    side = packed[:, 2 * head_size : 2 * head_size + 4].astype(F32)
    inv_full = side[:, 0:1] + side[:, 1:2]
    inner_full = side[:, 2:3] + side[:, 3:4]
    d_first = mm_nt(d_projected_full, w_proj)
    d_source = d_middle + inv_full * d_first * gain_first - source * inner_full
    d_gain_first = jnp.sum(d_first * source * inv_full, axis=0)
    normed_first = (source * inv_full * gain_first).astype(BF)

    def attention_grads():
        owned = by_owner(d_projected_full, query_width, head_size, n_ctx)
        proj_grad = weight_grad(
            both_halves(section_id, *row_halves(owned, n_ctx)), both_sections(normed_first)
        )
        return [out_grad, proj_grad]

    return d_source, (down_kept, gate_up_kept), attention_grads, attention_kept, d_gain_first, d_gain_second


def both_sections(value):
    return jnp.concatenate([value, shift(value, "section", 1)], axis=0)


def both_halves(section_id, low, high):
    own = jnp.where(section_id == 0, low, high)
    other = jnp.where(section_id == 0, high, low)
    return jnp.concatenate([own, shift(other, "section", 1)], axis=0)


def row_halves(value, n_ctx):
    part = value.shape[1] // n_ctx
    half = part // 2
    return tuple(
        jnp.concatenate([value[:, c * part + h * half : c * part + (h + 1) * half] for c in range(n_ctx)], axis=1)
        for h in range(2)
    )


def by_owner(value, query_width, head_size, n_ctx):
    query_part = query_width // n_ctx
    head_part = head_size // n_ctx
    pieces = []
    for c in range(n_ctx):
        pieces.append(value[:, c * query_part : (c + 1) * query_part])
        for base in (query_width, query_width + head_size):
            pieces.append(value[:, base + c * head_part : base + (c + 1) * head_part])
    return jnp.concatenate(pieces, axis=1)


def weight_grad(left, right):
    return natural(mm_tn(left, right).astype(BF))


def keep(*partials):
    n_ctx = lax.axis_size("ctx")
    return lax.psum_scatter(stack_rows(partials, n_ctx), "ctx", scatter_dimension=0, tiled=True)


def stack_rows(partials, n_ctx):
    if len(partials) == 1:
        return partials[0]
    blocks = [partial.reshape(n_ctx, -1, partial.shape[1]) for partial in partials]
    return jnp.concatenate(blocks, axis=1).reshape(-1, partials[0].shape[1])


def home(section_id, first_block, second_block):
    kept = jnp.where(section_id == 0, first_block, second_block)
    sent = jnp.where(section_id == 0, second_block, first_block)
    received = shift(sent, "section", 1)
    low = jnp.where(section_id == 0, kept, received)
    high = jnp.where(section_id == 0, received, kept)
    return low, high


def local(hidden_in, out_grad, block_pos, norm1_gain, norm2_gain, wq, wk, wv, wo, w_gate, w_up, w_down):
    n_section = lax.axis_size("section")
    assert n_section == 2
    n_ctx = lax.axis_size("ctx")
    section_id = lax.axis_index("section")
    micro_count, row_count, width = hidden_in.shape
    micro_own = micro_count // n_section
    query_width = wq.shape[2]
    head_size = wk.shape[2]

    def fetch(weight):
        return lax.all_gather(weight, "section", axis=0, tiled=False)

    def fetch_fast(weight):
        received = shift(weight, "section", 1)
        return lax.optimization_barrier(
            (jnp.where(section_id == 0, weight, received), jnp.where(section_id == 0, received, weight))
        )

    gains = jnp.concatenate([norm1_gain, norm2_gain], axis=0)
    other_gains = shift(gains, "section", 1)
    other_proj = jnp.concatenate(
        [shift(wq[0], "section", 1), shift(jnp.concatenate([wk[0], wv[0]], axis=1), "section", 1)], axis=1
    )
    own_proj = jnp.concatenate([wq[0], wk[0], wv[0]], axis=1)
    other_proj, other_gains, w_down_late = lax.optimization_barrier((other_proj, other_gains, w_down[0]))
    w_proj = lax.optimization_barrier(
        (jnp.where(section_id == 0, own_proj, other_proj), jnp.where(section_id == 0, other_proj, own_proj))
    )
    weights = (w_proj, fetch(wo[0]), fetch(w_gate[0]), fetch(w_up[0]), fetch_fast(w_down_late))
    gains = [jnp.where(section_id == 0, gains, other_gains), jnp.where(section_id == 0, other_gains, gains)]
    second_full = []

    def gather_second(partial):
        own, partial = lax.optimization_barrier((jnp.stack([gains[0][1], gains[1][1]]), partial))
        second_full.append(gather_cols(own, "wt"))
        return partial, second_full[0][0]

    params = [[gains[l][0], gather_second] + [w[l] for w in weights] for l in range(n_section)]
    first_micro = section_id * micro_own
    layout = Layout(block_pos, first_micro, micro_own, row_count)

    def own_rows(value):
        return lax.dynamic_slice_in_dim(value, first_micro, micro_own, 0).reshape(micro_own * row_count, width)

    cotangent = own_rows(out_grad)
    state, saved_0, grad_full = layer_forward(
        own_rows(hidden_in).astype(F32), layout, params[0], cotangent, [params[0][6]]
    )
    for l in range(n_section):
        params[l][1] = second_full[0][l]
    update, saved_1, _ = layer_forward(state, layout, params[1], last=True)
    grad, feed_1, pending, _, d_first_1, d_second_1 = layer_backward(
        cotangent.astype(F32), grad_full, layout, saved_1, params[1]
    )
    in_grad_own, feed_0, pending, attention_1, d_first_0, d_second_0 = layer_backward(
        grad, None, layout, saved_0, params[0], (pending, feed_1[1])
    )
    joined = stack_rows(pending(), n_ctx)
    gain_sum = jnp.stack([jnp.stack([d_first_0, d_second_0]), jnp.stack([d_first_1, d_second_1])])
    update, gain_sum, in_grad_own = after([update, gain_sum, in_grad_own], [joined])
    parts = send_rows(joined, "ctx") + send_cols(update, "wt")
    parts = lax.optimization_barrier(tuple(parts))
    attention_0 = add_up(parts[:n_ctx]).astype(BF)
    out_own = (saved_1[8] + add_up(parts[n_ctx:])).astype(BF)
    feed_0 = after(feed_0, [attention_0])

    def everywhere(own):
        low, high = own, shift(own, "section", 1)
        both = jnp.concatenate(
            [jnp.where(section_id == 0, low, high), jnp.where(section_id == 0, high, low)], axis=0
        )
        return both.reshape(micro_count, row_count, width)

    out = everywhere(out_own)
    in_grad = everywhere(in_grad_own)
    gain_sum = gain_sum + shift(gain_sum, "section", 1)
    gain_sum = sum_in_order(gain_sum, "ctx")
    gain_mine = jnp.where(section_id == 0, gain_sum[0], gain_sum[1])
    down, gate_up = (home(section_id, a, b) for a, b in zip(feed_0, feed_1))
    grad_down = jnp.concatenate(down, axis=0).T.astype(F32)
    grad_gate, grad_up = (half.astype(F32) for half in gate_up)
    low, high = home(section_id, attention_0, attention_1)
    out_rows = query_width // n_ctx // 2
    grad_wo = jnp.concatenate([low[:out_rows], high[:out_rows]], axis=0).astype(F32)
    grad_proj = jnp.concatenate([low[out_rows:], high[out_rows:]], axis=0).T.astype(F32)
    query_part = query_width // n_ctx
    head_part = head_size // n_ctx
    return (
        out,
        in_grad,
        grad_proj[:, :query_part][None],
        grad_proj[:, query_part : query_part + head_part][None],
        grad_proj[:, query_part + head_part :][None],
        grad_wo[None],
        grad_gate[None],
        grad_up[None],
        grad_down[None],
        gain_mine[0][None],
        gain_mine[1][None],
    )


def solution(mesh):
    return jax.shard_map(
        local,
        mesh=mesh,
        in_specs=(
            P(None, "ctx", "wt"),
            P(None, "ctx", "wt"),
            P(),
            P("section", "wt"),
            P("section", "wt"),
            P("section", "wt", None),
            P("section", "wt", None),
            P("section", "wt", None),
            P("section", None, "wt"),
            P("section", None, "wt"),
            P("section", None, "wt"),
            P("section", "wt", None),
        ),
        out_specs=(
            P(None, "ctx", "wt"),
            P(None, "ctx", "wt"),
            P("section", "wt", "ctx"),
            P("section", "wt", "ctx"),
            P("section", "wt", "ctx"),
            P("section", "ctx", "wt"),
            P("section", "ctx", "wt"),
            P("section", "ctx", "wt"),
            P("section", "wt", "ctx"),
            P("section", "wt"),
            P("section", "wt"),
        ),
        check_vma=False,
    )
```
